32 devices in a mesh: groups: 2 (over y), context: 8 (over z, x), tensor: 2 (over core).
Axes of the slice: x: 2, y: 2, z: 4, core: 2. Of those that a mesh axis runs over, the one named last changes fastest.
Arguments:
- q_raw: bfloat16 [2048, 1024], P(('groups', 'context'), 'tensor'), parts along dimension 0, may hold values from -6 to 6
- k_raw: bfloat16 [2048, 1024], P(('groups', 'context'), 'tensor'), parts along dimension 0, may hold values from -6 to 6
- v_raw: bfloat16 [2048, 2048], P(('groups', 'context'), 'tensor'), parts along dimension 0, may hold values from -6 to 6
- gate_z: bfloat16 [2048, 2048], P(('groups', 'context'), 'tensor'), parts along dimension 0, may hold values from -6 to 6
- beta_logit: float32 [2048, 16], P(('groups', 'context'), 'tensor'), parts along dimension 0
- decay_in: float32 [2048, 16], P(('groups', 'context'), 'tensor'), parts along dimension 0
- conv_q: bfloat16 [4, 1024], P(None, 'tensor'), may hold values from -3 to 3
- conv_k: bfloat16 [4, 1024], P(None, 'tensor'), may hold values from -3 to 3
- conv_v: bfloat16 [4, 2048], P(None, 'tensor'), may hold values from -3 to 3
- a_log: float32 [16], P('tensor'), may hold values from 0 to 1.1
- dt_bias: float32 [16], P('tensor'), may hold values from -0.5 to 0.5
- norm_gain: float32 [128], replicated, may hold values from 0.25 to 1.75
Outputs:
- mixed_out: bfloat16 [2048, 2048], P(('groups', 'context'), 'tensor'), parts along dimension 0
The draws below stay inside these ranges and needn't reach their ends.
There are 2 independent parts, one for each index of `groups`. The reference program is written for one: setup_inputs(seed, part) draws one part's arguments, and reference() takes and returns one part's arrays. A program takes and returns all parts, laid end to end along the dimension named above; an argument that names none is the same for every part. Nothing has to cross between parts.
All inputs are finite; a program needn't handle non-finite values.
Results may differ from the reference program's by a relative error of at most 0.0085.
Values may be sent and summed in bfloat16 or wider, within the bound.
A program may use at most 256 MiB of HBM per device.

```python
import jax
import jax.numpy as jnp
from jax import lax

TOK_DEV = 128
HK = 8
HV = 16
DK = 128
CONV = 4
SPAN = 64
TOKENS = 1024


def head_plan(key):
    marked = jax.random.fold_in(key, 11)
    head_order = jax.random.permutation(jax.random.fold_in(marked, 1), HV)
    family = head_order % 5
    low_end = 0.5
    strength_level = jax.random.uniform(jax.random.fold_in(marked, 2), (HV,), minval=low_end, maxval=1.0)
    return (family, strength_level)


def block_plan(key):
    blocks = TOKENS // TOK_DEV
    marked = jax.random.fold_in(key, 13)
    narrow_shift = jax.random.uniform(jax.random.fold_in(marked, 1), (blocks, HV), minval=-0.7, maxval=0.7)
    broad_shift = jax.random.uniform(jax.random.fold_in(marked, 2), (blocks, HV), minval=-1.0, maxval=1.0)
    quiet_score = jax.random.uniform(jax.random.fold_in(marked, 3), (blocks, HV))
    narrow_rows = jnp.repeat(narrow_shift, TOK_DEV, axis=0)
    broad_rows = jnp.repeat(broad_shift, TOK_DEV, axis=0)
    quiet_rows = jnp.repeat(quiet_score, TOK_DEV, axis=0) < 0.5
    return (narrow_rows, broad_rows, quiet_rows)


def pick_family(family, parts):
    result = parts[0]
    for index in range(1, 5):
        result = jnp.where((family == index)[None, :], parts[index], result)
    return result


def draw_beta_logit(key, part):
    family, strength_level = head_plan(key)
    narrow_rows, broad_rows, quiet_rows = block_plan(key)
    jitter = jax.random.uniform(jax.random.fold_in(key, 21), (TOKENS, HV), minval=-1.0, maxval=1.0)
    fast_part = 3.0 * jitter
    lagging_part = jnp.log(strength_level * 40.0 / TOKENS)[None, :] + 0.5 * jitter
    spread_part = jitter
    faint_part = -6.0 + 0.5 * jitter
    switch_part = jnp.where(quiet_rows, faint_part, fast_part)
    result = pick_family(family, (fast_part, lagging_part, spread_part, faint_part, switch_part))
    return result.astype(jnp.float32)


def draw_decay_in(key, part):
    family, strength_level = head_plan(key)
    narrow_rows, broad_rows, quiet_rows = block_plan(key)
    jitter = jax.random.uniform(jax.random.fold_in(key, 31), (TOKENS, HV), minval=-1.0, maxval=1.0)
    fast_part = -4.6 + narrow_rows + jitter
    lagging_part = jnp.log(strength_level * 0.15 / TOKENS)[None, :] + narrow_rows + 0.5 * jitter
    sampled_locations = jax.random.randint(jax.random.fold_in(key, 33), (2, HV), 0, TOKENS)
    sequence_indices = jnp.arange(TOKENS)[:, None]
    sudden_entries = (sequence_indices == sampled_locations[0][None, :]) | (sequence_indices == sampled_locations[1][None, :])
    lagging_part = jnp.where(sudden_entries, -1.6 + 0.3 * jitter, lagging_part)
    relay_part = jnp.log(1.5 / TOK_DEV) + broad_rows + 0.3 * jitter
    switch_part = jnp.where(quiet_rows, -12.0 + jitter, -3.5 + 0.5 * jitter)
    result = pick_family(family, (fast_part, lagging_part, lagging_part, relay_part, switch_part))
    return result.astype(jnp.float32)


def block_scale(stream_key, dims, cuts, low, top_value):
    loudness, own = 1.0, jax.random.fold_in(stream_key, 6)
    for axis_at, blocks in cuts:
        heights = jnp.exp(jax.random.uniform(jax.random.fold_in(own, axis_at), (blocks,), jnp.float32, low / len(cuts), top_value / len(cuts)))
        loudness = loudness * jnp.repeat(heights, dims[axis_at] // blocks).reshape([-1 if axis == axis_at else 1 for axis in range(len(dims))])
    return loudness


def gaussian(stream_key, shape, deviation, most, pieces=(), kind=jnp.bfloat16):
    gain = block_scale(stream_key, shape, pieces, -0.22, 0.18) if pieces else 1.0
    values = jax.random.normal(stream_key, shape, jnp.float32) * deviation * gain
    return jnp.minimum(jnp.maximum(values, -most), most).astype(kind)


def setup_inputs(seed: int = 0, part: int = 0) -> dict:
    seeds = jax.random.split(jax.random.key(seed), 13)
    part_splits = jax.random.split(jax.random.fold_in(seeds[12], part), 13)
    q_raw = gaussian(part_splits[0], (TOKENS, HK * DK), 1.0, 6.0, ((0, 8), (1, 2)))
    k_raw = gaussian(part_splits[1], (TOKENS, HK * DK), 1.0, 6.0, ((0, 8), (1, 2)))
    v_raw = gaussian(part_splits[2], (TOKENS, HV * DK), 1.0, 6.0, ((0, 8), (1, 2)))
    gate_z = gaussian(part_splits[3], (TOKENS, HV * DK), 1.0, 6.0, ((0, 8), (1, 2)))
    beta_logit = draw_beta_logit(jax.random.fold_in(jax.random.fold_in(seeds[12], part), 71), part)
    decay_in = draw_decay_in(jax.random.fold_in(jax.random.fold_in(seeds[12], part), 71), part)
    conv_q = gaussian(seeds[6], (CONV, HK * DK), CONV ** -0.5, 3.0, ((1, 2),))
    conv_k = gaussian(seeds[7], (CONV, HK * DK), CONV ** -0.5, 3.0, ((1, 2),))
    conv_v = gaussian(seeds[8], (CONV, HV * DK), CONV ** -0.5, 3.0, ((1, 2),))
    a_log = jnp.clip(1.1 * jax.random.uniform(seeds[9], (HV,), jnp.float32) ** block_scale(seeds[9], (HV,), ((0, 2),), -0.2, 0.2), 0.0, 1.1)
    dt_bias = jnp.clip(jax.random.uniform(seeds[10], (HV,), jnp.float32, -0.5, 0.5) * block_scale(seeds[10], (HV,), ((0, 2),), -0.4, 0.0), -0.5, 0.5)
    norm_gain = jnp.clip(1.0 + 0.15 * jax.random.normal(seeds[11], (DK,), jnp.float32), 0.25, 1.75)
    return {"q_raw": q_raw, "k_raw": k_raw, "v_raw": v_raw, "gate_z": gate_z, "beta_logit": beta_logit, "decay_in": decay_in, "conv_q": conv_q, "conv_k": conv_k, "conv_v": conv_v, "a_log": a_log, "dt_bias": dt_bias, "norm_gain": norm_gain}


HIGH = lax.Precision.HIGHEST

def mixing_weight(form, left, right):
    return jnp.einsum(form, left, right, precision=HIGH)

def causal_conv(rows, rim, weights):
    full = jnp.concatenate([rim, rows], axis=0).astype(jnp.float32)
    taps = weights.shape[0]
    count = rows.shape[0]
    total = jnp.zeros((count, rows.shape[1]), jnp.float32)
    for place in range(taps):
        total = total + weights[place].astype(jnp.float32)[None, :] * full[place:place + count]
    return jax.nn.silu(total).astype(jnp.bfloat16)

def prepare(query_rows, key_rows, value_rows, beta_logit, decay_in, a_log, dt_bias, size):
    rows = query_rows.shape[0]
    kheads = query_rows.shape[1] // size
    vheads = value_rows.shape[1] // size
    repeat = vheads // kheads

    def unit(block):
        block = block.astype(jnp.float32).reshape(rows, kheads, size)
        block = block / jnp.sqrt(lax.optimization_barrier(jnp.sum(block * block, axis=-1, keepdims=True)) + 1e-06)
        return jnp.repeat(block, repeat, axis=1)
    q_unit = unit(query_rows) * size ** (-0.5)
    k_unit = unit(key_rows)
    v_full = value_rows.astype(jnp.float32).reshape(rows, vheads, size)
    betas = jax.nn.sigmoid(beta_logit)
    decays = -jnp.exp(a_log)[None, :] * jax.nn.softplus(decay_in + dt_bias[None, :])
    return (q_unit, k_unit, v_full, betas, decays)

def to_blocks(array, span):
    count = array.shape[0] // span
    array = array.reshape((count, span) + array.shape[1:])
    return jnp.swapaxes(array, 1, 2)

def unpack_segments(array):
    array = jnp.swapaxes(array, 1, 2)
    return array.reshape((array.shape[0] * array.shape[1],) + array.shape[2:])

def span_parts(query_rows, key_rows, betas, decays):
    count = decays.shape[-1]
    cumul = jnp.cumsum(decays, axis=-1)
    place = jnp.arange(count)
    later = place[:, None] >= place[None, :]
    strict = place[:, None] > place[None, :]
    gap = cumul[:, :, None] - cumul[:, None, :]
    ratio = jnp.where(later[None], jnp.exp(jnp.minimum(gap, 0.0)), 0.0)
    inner = mixing_weight('hck,hdk->hcd', key_rows, key_rows)
    lower = jnp.where(strict[None], betas[:, :, None] * ratio * inner, 0.0)
    system = lower + jnp.eye(count, dtype=jnp.float32)[None]
    score_matrix = mixing_weight('hck,hdk->hcd', query_rows, key_rows) * ratio
    growth_factor = jnp.exp(cumul)
    tail_tokens = jnp.exp(cumul[:, -1:] - cumul)
    return (system, score_matrix, growth_factor, tail_tokens)

def solve_lower(system, rhs):
    count = system.shape[-1]
    unit_matrix = jnp.eye(count, dtype=system.dtype)[None]
    power = unit_matrix - system
    inverse = unit_matrix + power
    levels = (count - 1).bit_length()
    for level in range(1, levels):
        power = mixing_weight('hij,hjk->hik', power, power)
        inverse = inverse + mixing_weight('hij,hjk->hik', inverse, power)
    return mixing_weight('hij,hjk->hik', inverse, rhs)

def span_apply(state_matrix, inputs):
    query_rows, key_rows, value_rows, betas, decays = inputs
    system, score_matrix, growth_factor, tail_tokens = span_parts(query_rows, key_rows, betas, decays)
    known_prefix = value_rows - growth_factor[:, :, None] * mixing_weight('uxz,uzn->uxn', key_rows, state_matrix)
    state_update = solve_lower(system, betas[:, :, None] * known_prefix)
    output_rows = growth_factor[:, :, None] * mixing_weight('uxz,uzn->uxn', query_rows, state_matrix) + mixing_weight('jpr,jrf->jpf', score_matrix, state_update)
    last_token = growth_factor[:, -1][:, None, None]
    updated_state = last_token * state_matrix + mixing_weight('rbe,rbi->rei', key_rows, tail_tokens[:, :, None] * state_update)
    return (updated_state, output_rows)

def finish(mixed, gate_z, norm_gain):
    rows = mixed.shape[0]
    scale = jnp.sqrt(lax.optimization_barrier(jnp.mean(mixed * mixed, axis=-1, keepdims=True)) + 1e-06)
    gate = gate_z.astype(jnp.float32).reshape(mixed.shape)
    result = mixed / scale * norm_gain[None, None, :] * jax.nn.silu(gate)
    return result.reshape(rows, -1).astype(jnp.bfloat16)

def reference(q_raw, k_raw, v_raw, gate_z, beta_logit, decay_in, conv_q, conv_k, conv_v, a_log, dt_bias, norm_gain):
    size = norm_gain.shape[0]
    taps = conv_q.shape[0]
    query_rows = causal_conv(q_raw, jnp.zeros((taps - 1, q_raw.shape[1]), jnp.bfloat16), conv_q)
    key_rows = causal_conv(k_raw, jnp.zeros((taps - 1, k_raw.shape[1]), jnp.bfloat16), conv_k)
    value_rows = causal_conv(v_raw, jnp.zeros((taps - 1, v_raw.shape[1]), jnp.bfloat16), conv_v)
    prepared = prepare(query_rows, key_rows, value_rows, beta_logit, decay_in, a_log, dt_bias, size)
    inputs = tuple((to_blocks(array, SPAN) for array in prepared))
    heads = prepared[2].shape[1]
    state_matrix = jnp.zeros((heads, size, size), jnp.float32)
    final, mixer_results = lax.scan(span_apply, state_matrix, inputs)
    return finish(unpack_segments(mixer_results), gate_z, norm_gain)
```

```python
import functools
import math

import jax
import jax.numpy as jnp
from jax import lax
from jax.experimental import pallas as pl
from jax.experimental.pallas import tpu as pltpu
from jax.sharding import PartitionSpec as P

MESH = pl.DeviceIdType.MESH
HIGH = lax.Precision.HIGHEST
RIM = 16
BF = jnp.bfloat16
F32 = jnp.float32
CROSS = False


def mm(a, b):
    return jnp.dot(a.astype(BF), b.astype(BF), preferred_element_type=F32)


def mm_nt(a, b):
    return lax.dot_general(a.astype(BF), b.astype(BF), (((1,), (1,)), ((), ())), preferred_element_type=F32)


def mm_tn(a, b):
    return jnp.dot(a.astype(BF).T, b.astype(BF), preferred_element_type=F32)


def conv_silu(full, weights, count):
    taps = weights.shape[0]
    total = weights[0:1].astype(F32) * full(0)
    for i in range(1, taps):
        total = total + weights[i : i + 1].astype(F32) * full(i)
    return (total * jax.nn.sigmoid(total)).astype(BF)


def norm(block):
    block = block.astype(F32)
    return 1.0 / jnp.sqrt(jnp.sum(block * block, axis=-1, keepdims=True) + 1e-06)


def masks(rows):
    row = lax.broadcasted_iota(jnp.int32, (rows, rows), 0)
    col = lax.broadcasted_iota(jnp.int32, (rows, rows), 1)
    return row, col


def key_stage(ks, beta, decays, repeat):
    rows = ks[0].shape[0]
    units = beta.shape[1]
    row, col = masks(rows)
    kn = [norm(k) for k in ks]
    kn_rows = jnp.zeros((rows, rows), F32)
    for j, column in enumerate(kn):
        kn_rows = jnp.where(col == j, column, kn_rows)
    kn_rows = kn_rows.T
    inner = [mm_nt(k, k) for k in ks]
    lower, ratios = [], []
    for h in range(units):
        j = h // repeat
        ratio = decays[h] * kn_rows[j : j + 1]
        lower.append(jnp.where(row > col, ratio * inner[j] * (beta[:, h : h + 1] * kn[j]), 0.0))
        ratios.append(ratio)
    eye = (row == col).astype(F32)
    apart = row ^ col
    inv, rest = [], []
    for m in lower:
        edge, full = jnp.where(apart == 1, m, 0.0), m + eye
        inv.append(eye - edge)
        rest.append(full - mm(edge, full))
    step = 2
    while step < rows:
        mask = (apart >= step) & (apart < 2 * step)
        for h in range(units):
            edge = jnp.where(mask, rest[h], 0.0)
            if 2 * step < rows:
                both = mm(edge, jnp.concatenate([inv[h].astype(BF), rest[h].astype(BF)], axis=1))
                inv[h], rest[h] = inv[h] - both[:, :rows], rest[h] - both[:, rows:]
            else:
                inv[h] = inv[h] - mm(edge, inv[h])
        step *= 2
    return kn, kn_rows, ratios, inv


def mixer_kernel(
    axis, n, side, team, size,
    q_ref, k_ref, v_ref, bl_ref, di_ref, wq_ref, wk_ref, wv_ref, al_ref, dt_ref, gain_ref,
    out_ref,
    q_rows, k_rows, v_rows, logits, gates, seen, taps_s, scales, gain,
    fq, fk, fv, m_s, g_s, b_s, r_s, w_s, s_s, p_s, o_s, held, sent, back,
    local_sem, send_sem, recv_sem, rim_send, hop_send, hop_recv, back_send, back_recv, rim_ready, hop_ready,
):
    me = lax.axis_index(axis)
    place, turn = lax.rem(me, team), me // team
    base = turn * team
    rows = q_ref.shape[0]
    taps = wq_ref.shape[0]
    kw, vw = wq_ref.shape[1] // team, wv_ref.shape[1] // team
    kpm, hpm = kw // size, vw // size
    repeat = hpm // kpm
    units = team * hpm
    first, last = turn == 0, turn == n // team - 1
    tail_place = place == team - 1
    feeds_rim = tail_place & jnp.logical_not(last)
    streams = ((k_ref, k_rows, kw), (v_ref, v_rows, vw), (q_ref, q_rows, kw))
    plans = ((k_rows, 0, fk, kpm), (v_rows, kpm, fv, hpm), (q_rows, kpm + hpm, fq, kpm))
    GATES, TAPS = 3, 4
    other = None if side is None else 1 - lax.axis_index(side)
    if team == 4:
        order = [3 - place, lax.rem(place + 2, team), place + 1 - 2 * lax.rem(place, 2), place]
    else:
        order = [lax.rem(place + d, team) for d in range(1, team)] + [place]
    away = order if side is not None else order[:-1]

    def across(who):
        return {axis: who} if side is None else {axis: who, side: other}

    def lanes_of(who, width):
        return pl.ds(pl.multiple_of(who * width, width), width)

    def rows_of(who):
        return pl.ds(pl.multiple_of(RIM + who * rows, RIM), rows)

    def remote(src, dst, send, recv, to):
        return pltpu.make_async_remote_copy(
            src_ref=src, dst_ref=dst, send_sem=send, recv_sem=recv, device_id=to, device_id_type=MESH
        )

    def share(src, dst, i, who):
        if side is None:
            @pl.when(who == place)
            def _():
                pltpu.make_async_copy(src, dst, recv_sem.at[i]).start()

            @pl.when(who != place)
            def _():
                remote(src, dst, send_sem.at[i], recv_sem.at[i], across(base + who)).start()
        else:
            remote(src, dst, send_sem.at[i], recv_sem.at[i], across(base + who)).start()

    def spread(i):
        src, dst, width = streams[i]
        for who in away:
            remote(
                src.at[:, lanes_of(who, width)], dst.at[rows_of(place), :],
                send_sem.at[i], recv_sem.at[i], across(base + who),
            ).start()

    def tap_pieces():
        pieces = []
        at = 0
        for ref, count in ((wk_ref, kpm), (wv_ref, hpm), (wq_ref, kpm)):
            for c in range(count):
                lanes = pl.ds(pl.multiple_of((place * count + c) * size, size), size)
                pieces.append((ref.at[:, lanes], taps_s.at[at]))
                at += 1
        return pieces

    loads = [
        (bl_ref, logits.at[0], 0), (di_ref, logits.at[1], 0), (al_ref, scales.at[0], 1), (dt_ref, scales.at[1], 1),
        (gain_ref, gain, 2),
    ]
    for src, dst, i in loads:
        pltpu.make_async_copy(src, dst, local_sem.at[i]).start()
    if side is None:
        for i, (src, dst, width) in enumerate(streams):
            pltpu.make_async_copy(src.at[:, lanes_of(place, width)], dst.at[rows_of(place), :], recv_sem.at[i]).start()
        for src, dst in tap_pieces():
            pltpu.make_async_copy(src, dst, recv_sem.at[TAPS]).start()

    barrier = pltpu.get_barrier_semaphore()

    def greet(to):
        pl.semaphore_signal(barrier, inc=1, device_id=to, device_id_type=MESH)

    for who in away:
        greet(across(base + who))

    @pl.when(jnp.logical_not(last))
    def _():
        greet({axis: me + team})

    @pl.when(feeds_rim)
    def _():
        for p in range(team):
            greet(across(base + team + p))

    pl.semaphore_wait(barrier, len(away) + jnp.where(first, 0, 2))
    spread(0)
    if side is not None:
        for src, dst in tap_pieces():
            remote(src, dst, send_sem.at[TAPS], recv_sem.at[TAPS], across(me)).start()

    @pl.when(jnp.logical_not(first))
    def _():
        pl.semaphore_signal(rim_ready, inc=1, device_id=across(base - 1), device_id_type=MESH)
        pl.semaphore_signal(hop_ready, inc=1, device_id={axis: me - team}, device_id_type=MESH)

    pltpu.make_async_copy(logits, logits, local_sem.at[0]).wait()
    pltpu.make_async_copy(scales, scales, local_sem.at[1]).wait()
    heads = bl_ref.shape[0]
    diag = lax.broadcasted_iota(jnp.int32, (heads, heads), 0) == lax.broadcasted_iota(jnp.int32, (heads, heads), 1)

    def upright(row):
        return jnp.sum(jnp.where(diag, row, 0.0), axis=1, keepdims=True)

    row, col = masks(rows)
    x = logits[1] + upright(scales[1])
    decay = -jnp.exp(upright(scales[0])) * (jnp.maximum(x, 0.0) + jnp.log1p(jnp.exp(-jnp.abs(x))))
    cum = jnp.dot(decay, (row <= col).astype(F32), precision=HIGH, preferred_element_type=F32)
    beta = jax.nn.sigmoid(logits[0])
    for p in range(team):
        gates[p, pl.ds(0, hpm), :] = cum[p * hpm : (p + 1) * hpm]
        gates[p, pl.ds(hpm, hpm), :] = beta[p * hpm : (p + 1) * hpm]
    for who in order:
        share(gates.at[who], seen.at[place], GATES, who)
    spread(1)

    def rim(p, i):
        src, dst, width = streams[i]
        return remote(
            src.at[pl.ds(rows - RIM, RIM), pl.ds(p * width, width)], dst.at[pl.ds(0, RIM), :],
            rim_send.at[i], recv_sem.at[i], across(base + team + p),
        )

    @pl.when(feeds_rim)
    def _():
        pl.semaphore_wait(rim_ready, team)
        for i in range(len(streams)):
            for p in range(team):
                rim(p, i).start()

    @pl.when(first)
    def _():
        for _, dst, _ in streams:
            dst[pl.ds(0, RIM), :] = jnp.zeros((RIM, dst.shape[1]), BF)

    def arrived(ref, i):
        pltpu.make_async_copy(ref, ref, recv_sem.at[i]).wait()

    def stream(i):
        src, at, f_ref, count = plans[i]

        @pl.when(first)
        def _():
            arrived(src.at[pl.ds(RIM, team * rows), :], i)

        @pl.when(jnp.logical_not(first))
        def _():
            arrived(src, i)

        if i == 0:
            spread(2)
        f_ref[...] = src[...].astype(F32)
        parts = []
        for b in range(team):
            for c in range(count):
                lanes = pl.ds(c * size, size)
                parts.append(
                    conv_silu(
                        lambda i: f_ref[pl.ds(RIM - taps + 1 + i + b * rows, rows), lanes], taps_s[at + c], rows
                    )
                )
        return parts

    arrived(seen, GATES)
    cum_rows = jnp.concatenate([seen[b, pl.ds(0, hpm), :] for b in range(team)], axis=0)
    beta_rows = jnp.concatenate([seen[b, pl.ds(hpm, hpm), :] for b in range(team)], axis=0)
    pad = jnp.zeros((rows - 2 * units, rows), F32)
    columns = jnp.concatenate([cum_rows, beta_rows, pad], axis=0).T
    cum, beta = columns[:, :units], columns[:, units : 2 * units]
    growth = jnp.exp(cum)
    tail = jnp.exp(cum[rows - 1 : rows] - cum)
    for u in range(units):
        ratio = jnp.exp(jnp.minimum(cum[:, u : u + 1] - cum_rows[u : u + 1], 0.0))
        r_s[u] = jnp.where(row >= col, ratio, 0.0)
    arrived(taps_s, TAPS)
    ks = stream(0)
    kn, kn_rows, ratios, inv = key_stage(ks, beta, [r_s[u] for u in range(units)], repeat)
    for u in range(units):
        r_s[u] = ratios[u]
        beta_row = beta_rows[u : u + 1]
        gain_row = beta_row * jnp.exp(cum_rows[u : u + 1]) * kn_rows[u // repeat : u // repeat + 1]
        w_s[u, :, pl.ds(0, size)] = mm(inv[u] * gain_row, ks[u // repeat]).astype(BF)
    inv = [(inv[u] * beta_rows[u : u + 1]).astype(BF) for u in range(units)]
    vs = stream(1)
    for u in range(units):
        w_s[u, :, pl.ds(size, size)] = mm(inv[u], vs[u]).astype(BF)
    for u in range(units):
        key_tail = (ks[u // repeat].astype(F32) * (kn[u // repeat] * tail[:, u : u + 1])).astype(BF)
        ends = mm_tn(key_tail, w_s[u])
        m_s[u] = (-ends[:, :size]).astype(BF)
        b_s[u] = ends[:, size:]
        g_s[pl.ds(u, 1), :] = jnp.broadcast_to(growth[rows - 1 : rows, u : u + 1], (1, size))

    def hop(h, to):
        return remote(sent.at[h], held.at[h], hop_send, hop_recv.at[h], {axis: to})

    def onward(states):
        @pl.when(jnp.logical_not(last))
        def _():
            for h in range(hpm):
                sent[h] = states[h].astype(BF)
                if h == 0:
                    pl.semaphore_wait(hop_ready, 1)
                hop(h, me + team).start()

    @pl.when(first)
    def _():
        states = [b_s[h] for h in range(hpm)]
        for h in range(hpm):
            s_s[h] = jnp.zeros((size, size), BF)
        for b in range(1, team):
            for h in range(hpm):
                u = b * hpm + h
                low = states[h].astype(BF)
                s_s[u] = low
                states[h] = (
                    b_s[u] + g_s[pl.ds(u, 1), :] * states[h] + jnp.dot(m_s[u], low, preferred_element_type=F32)
                )
        onward(states)

    qs = stream(2)
    cross = [mm_nt(q, k) for q, k in zip(qs, ks)]
    qn = [norm(q) * size ** (-0.5) for q in qs]
    for u in range(units):
        j = u // repeat
        inside = mm(r_s[u] * cross[j] * qn[j], w_s[u])
        p_s[u] = (qs[j].astype(F32) * (qn[j] * growth[:, u : u + 1]) - inside[:, :size]).astype(BF)
        o_s[u] = inside[:, size:]

    @pl.when(jnp.logical_not(first))
    def _():
        row, col = masks(size)
        eye = (row == col).astype(F32)
        turns = [g_s[pl.ds(h, 1), :] * eye + m_s[h].astype(F32) for h in range(hpm)]
        adds = [b_s[h] for h in range(hpm)]
        for b in range(1, team):
            for h in range(hpm):
                u = b * hpm + h
                low = jnp.concatenate([turns[h].astype(BF), adds[h].astype(BF)], axis=1)
                end = g_s[pl.ds(u, 1), :]
                moved = jnp.dot(m_s[u], low, preferred_element_type=F32)
                viewed = jnp.dot(p_s[u], low, preferred_element_type=F32)
                p_s[u] = viewed[:, :size].astype(BF)
                o_s[u] = o_s[u] + viewed[:, size:]
                turns[h] = end * turns[h] + moved[:, :size]
                adds[h] = b_s[u] + end * adds[h] + moved[:, size:]
        for h in range(hpm):
            m_s[h] = turns[h].astype(BF)
            b_s[h] = adds[h]
        for h in range(hpm):
            hop(h, me - team).wait_recv()

        @pl.when(jnp.logical_not(last))
        def _():
            onward([b_s[h] + jnp.dot(m_s[h], held[h], preferred_element_type=F32) for h in range(hpm)])

        for u in range(units):
            s_s[u] = held[u % hpm]

    for b in order:
        for h in range(hpm):
            u = b * hpm + h
            mixed = o_s[u] + jnp.dot(p_s[u], s_s[u], preferred_element_type=F32)
            scale = lax.rsqrt(jnp.mean(mixed * mixed, axis=-1, keepdims=True) + 1e-06)
            if b is order[0] and h == 0:
                pltpu.make_async_copy(gain_ref, gain, local_sem.at[2]).wait()
            back[b, :, pl.ds(h * size, size)] = (mixed * scale * gain[...]).astype(BF)
        lanes = lanes_of(place, vw)
        if side is None and b is place:
            pltpu.make_async_copy(back.at[b], out_ref.at[:, lanes], back_recv).start()
        else:
            remote(back.at[b], out_ref.at[:, lanes], back_send, back_recv, across(base + b)).start()

    pltpu.make_async_copy(out_ref, out_ref, back_recv).wait()

    def gone(ref, sem):
        pltpu.make_async_copy(ref, ref, sem).wait()

    if away:
        gone(back.at[pl.ds(0, len(away))], back_send)
        gone(seen.at[pl.ds(0, len(away))], send_sem.at[GATES])
        for i, (_, dst, _) in enumerate(streams):
            gone(dst.at[pl.ds(RIM, len(away) * rows), :], send_sem.at[i])
    if side is not None:
        gone(taps_s, send_sem.at[TAPS])

    @pl.when(feeds_rim)
    def _():
        for i, (_, dst, _) in enumerate(streams):
            gone(dst.at[pl.ds(RIM, team * RIM), :], rim_send.at[i])

    @pl.when(jnp.logical_not(last))
    def _():
        gone(sent, hop_send)


def per_device(
    n, sides, q_raw, k_raw, v_raw, gate_z, beta_logit, decay_in, conv_q, conv_k, conv_v, a_log, dt_bias, norm_gain
):
    size = norm_gain.shape[0]
    rows, width = q_raw.shape
    vwidth = v_raw.shape[1]
    heads = vwidth // size
    taps = conv_q.shape[0]
    team = math.gcd(n, width // size)
    kw, vw = width // team, vwidth // team
    kpm, hpm = kw // size, vw // size
    units = team * hpm
    long = RIM + team * rows
    grows = -(-2 * hpm // 8) * 8
    dma = pltpu.SemaphoreType.DMA
    normed = pl.pallas_call(
        functools.partial(mixer_kernel, "context", n, "tensor" if CROSS and sides == 2 else None, team, size),
        out_shape=pltpu.VMEM((rows, vwidth), BF),
        in_specs=[pl.BlockSpec(memory_space=pltpu.HBM)] * 11,
        out_specs=pl.BlockSpec(memory_space=pltpu.VMEM),
        scratch_shapes=[
            pltpu.VMEM((long, kw), BF),
            pltpu.VMEM((long, kw), BF),
            pltpu.VMEM((long, vw), BF),
            pltpu.VMEM((2, heads, rows), F32),
            pltpu.VMEM((team, grows, rows), F32),
            pltpu.VMEM((team, grows, rows), F32),
            pltpu.VMEM((2 * kpm + hpm, taps, size), BF),
            pltpu.VMEM((2, 1, heads), F32),
            pltpu.VMEM((1, size), F32),
            pltpu.VMEM((long, kw), F32),
            pltpu.VMEM((long, kw), F32),
            pltpu.VMEM((long, vw), F32),
            pltpu.VMEM((units, size, size), BF),
            pltpu.VMEM((units, size), F32),
            pltpu.VMEM((units, size, size), F32),
            pltpu.VMEM((units, rows, rows), F32),
            pltpu.VMEM((units, rows, 2 * size), BF),
            pltpu.VMEM((units, size, size), BF),
            pltpu.VMEM((units, rows, size), BF),
            pltpu.VMEM((units, rows, size), F32),
            pltpu.VMEM((hpm, size, size), BF),
            pltpu.VMEM((hpm, size, size), BF),
            pltpu.VMEM((team, rows, vw), BF),
            dma((3,)),
            dma((5,)),
            dma((5,)),
            dma((3,)),
            dma,
            dma((hpm,)),
            dma,
            dma,
            pltpu.SemaphoreType.REGULAR,
            pltpu.SemaphoreType.REGULAR,
        ],
        compiler_params=pltpu.CompilerParams(
            collective_id=0, has_side_effects=True, vmem_limit_bytes=60 << 20
        ),
        name="mixer",
    )(
        q_raw, k_raw, v_raw, beta_logit.T, decay_in.T, conv_q, conv_k, conv_v,
        a_log[None], dt_bias[None], norm_gain[None],
    )
    return (normed.astype(F32) * jax.nn.silu(gate_z.astype(F32))).astype(BF)


def solution(mesh):
    rows = P(("groups", "context"), "tensor")
    return jax.shard_map(
        functools.partial(per_device, mesh.shape["context"], mesh.shape["tensor"]),
        mesh=mesh,
        in_specs=(rows,) * 6 + (P(None, "tensor"),) * 3 + (P("tensor"),) * 2 + (P(),),
        out_specs=rows,
        check_vma=False,
    )
```

```python
import functools
import math

import jax
import jax.numpy as jnp
from jax import lax
from jax.experimental import pallas as pl
from jax.experimental.pallas import tpu as pltpu
from jax.sharding import PartitionSpec as P

MESH = pl.DeviceIdType.MESH
HIGH = lax.Precision.HIGHEST
RIM = 16
BF = jnp.bfloat16
F32 = jnp.float32


def mm(a, b):
    return jnp.dot(a.astype(BF), b.astype(BF), preferred_element_type=F32)


def mm_nt(a, b):
    return lax.dot_general(a.astype(BF), b.astype(BF), (((1,), (1,)), ((), ())), preferred_element_type=F32)


def conv_silu(full, weights, count):
    taps = weights.shape[0]
    total = weights[0:1].astype(F32) * full(0)
    for i in range(1, taps):
        total = total + weights[i : i + 1].astype(F32) * full(i)
    return (total * jax.nn.sigmoid(total)).astype(BF)


def norm(block):
    block = block.astype(F32)
    return 1.0 / jnp.sqrt(jnp.sum(block * block, axis=-1, keepdims=True) + 1e-06)


def masks(rows):
    row = lax.broadcasted_iota(jnp.int32, (rows, rows), 0)
    col = lax.broadcasted_iota(jnp.int32, (rows, rows), 1)
    return row, col


def halves(a, step):
    parts = [a[i : i + step] for i in range(0, a.shape[0], step)]
    return jnp.concatenate(parts[::2], axis=0), jnp.concatenate(parts[1::2], axis=0)


def less(a, change, step):
    if change.shape[0] == a.shape[0]:
        return a - change
    parts = []
    for i in range(0, a.shape[0], 2 * step):
        parts += [a[i : i + step], a[i + step : i + 2 * step] - change[i // 2 : i // 2 + step]]
    return jnp.concatenate(parts, axis=0)


def key_stage(ks, beta, decays, repeat):
    rows = ks[0].shape[0]
    units = beta.shape[1]
    row, col = masks(rows)
    kn = [norm(k) for k in ks]
    kn_rows = jnp.zeros((rows, rows), F32)
    for j, column in enumerate(kn):
        kn_rows = jnp.where(col == j, column, kn_rows)
    kn_rows = kn_rows.T
    inner = [mm_nt(k, k) for k in ks]
    lower, ratios = [], []
    for h in range(units):
        j = h // repeat
        ratio = decays[h] * kn_rows[j : j + 1]
        lower.append(jnp.where(row > col, ratio * inner[j] * (beta[:, h : h + 1] * kn[j]), 0.0))
        ratios.append(ratio)
    eye = (row == col).astype(F32)
    apart = row ^ col
    inv, rest = [], []
    for m in lower:
        edge, full = jnp.where(apart == 1, m, 0.0), m + eye
        inv.append(eye - edge)
        rest.append(full - mm(edge, full))
    step = 2
    while step < rows:
        mask = (apart >= step) & (apart < 2 * step)
        for h in range(units):
            edge = jnp.where(mask, rest[h], 0.0)
            if step >= 8:
                edge = halves(edge, step)[1]
            if 2 * step < rows:
                both = mm(edge, jnp.concatenate([inv[h].astype(BF), rest[h].astype(BF)], axis=1))
                inv[h], rest[h] = less(inv[h], both[:, :rows], step), less(rest[h], both[:, rows:], step)
            else:
                inv[h] = less(inv[h], mm(edge, inv[h]), step)
        step *= 2
    return kn, kn_rows, ratios, inv


def mixer_kernel(
    axis, side, n, team, size,
    q_ref, k_ref, v_ref, bl_ref, di_ref, wq_ref, wk_ref, wv_ref, al_ref, dt_ref, gain_ref,
    out_ref,
    q_own, k_own, v_own, q_rows, k_rows, v_rows, logits, gates, seen, taps_s, scales, gain,
    fq, fk, fv, m_s, g_s, b_s, r_s, t_s, s_s, p_s, o_s, held, sent, back,
    local_sem, send_sem, recv_sem, rim_send, hop_send, hop_recv, back_send, back_recv, rim_ready, hop_ready,
):
    me = lax.axis_index(axis)
    place, turn = lax.rem(me, team), me // team
    base = turn * team
    rows = q_ref.shape[0]
    taps = wq_ref.shape[0]
    kw, vw = wq_ref.shape[1] // team, wv_ref.shape[1] // team
    kpm, hpm = kw // size, vw // size
    repeat = hpm // kpm
    units = team * hpm
    first, last = turn == 0, turn == n // team - 1
    tail_place = place == team - 1
    feeds_rim = tail_place & jnp.logical_not(last)
    streams = ((k_own, k_rows, kw), (v_own, v_rows, vw), (q_own, q_rows, kw))
    plans = ((k_rows, 0, fk, kpm), (v_rows, kpm, fv, hpm), (q_rows, kpm + hpm, fq, kpm))
    GATES, TAPS = 3, 4
    core = lax.axis_index(side)
    if team == 4:
        order = [3 - place, lax.rem(place + 2, team), place + 1 - 2 * lax.rem(place, 2), place]
    else:
        order = [lax.rem(place + d, team) for d in range(1, team)] + [place]
    away = order[:-1]

    def lanes_of(who, width):
        return pl.ds(pl.multiple_of(who * width, width), width)

    def rows_of(who):
        return pl.ds(pl.multiple_of(RIM + who * rows, RIM), rows)

    def remote(src, dst, send, recv, to):
        return pltpu.make_async_remote_copy(
            src_ref=src, dst_ref=dst, send_sem=send, recv_sem=recv, device_id=to, device_id_type=MESH
        )

    def loaded(i):
        pltpu.make_async_copy(streams[i][0], streams[i][0], local_sem.at[3 + i]).wait()

    def spread(i):
        src, dst, width = streams[i]
        if i < 2:
            loaded(i)
        for who in away:
            remote(
                src.at[:, lanes_of(who, width)], dst.at[rows_of(place), :],
                send_sem.at[i], recv_sem.at[i], {axis: base + who},
            ).start()
        pltpu.make_async_copy(src.at[:, lanes_of(place, width)], dst.at[rows_of(place), :], recv_sem.at[i]).start()

    def gone(ref, sem):
        pltpu.make_async_copy(ref, ref, sem).wait()

    def left(i):
        gone(streams[i][1].at[pl.ds(RIM, len(away) * rows), :], send_sem.at[i])

    def tap_pieces():
        pieces = []
        at = 0
        for ref, count in ((wk_ref, kpm), (wv_ref, hpm), (wq_ref, kpm)):
            for c in range(count):
                lanes = pl.ds(pl.multiple_of((place * count + c) * size, size), size)
                pieces.append((ref.at[:, lanes], taps_s.at[at]))
                at += 1
        return pieces

    loads = [
        (bl_ref, logits.at[0], 0), (di_ref, logits.at[1], 0), (al_ref, scales.at[0], 1), (dt_ref, scales.at[1], 1),
        (gain_ref, gain, 2), (k_ref, k_own, 3), (v_ref, v_own, 4), (q_ref, q_own, 5),
    ]
    barrier = pltpu.get_barrier_semaphore()

    def greet(to):
        pl.semaphore_signal(barrier, inc=1, device_id=to, device_id_type=MESH)

    for who in away:
        greet({axis: base + who})

    @pl.when(jnp.logical_not(last))
    def _():
        greet({axis: me + team})

    @pl.when(feeds_rim)
    def _():
        for p in range(team):
            greet({axis: base + team + p})

    for src, dst, i in loads:
        pltpu.make_async_copy(src, dst, local_sem.at[i]).start()
    for src, dst in tap_pieces():
        pltpu.make_async_copy(src, dst, recv_sem.at[TAPS]).start()

    pltpu.make_async_copy(logits, logits, local_sem.at[0]).wait()
    pltpu.make_async_copy(scales, scales, local_sem.at[1]).wait()
    heads = bl_ref.shape[0]
    diag = lax.broadcasted_iota(jnp.int32, (heads, heads), 0) == lax.broadcasted_iota(jnp.int32, (heads, heads), 1)

    def upright(row):
        return jnp.sum(jnp.where(diag, row, 0.0), axis=1, keepdims=True)

    row, col = masks(rows)
    x = logits[1] + upright(scales[1])
    decay = -jnp.exp(upright(scales[0])) * (jnp.maximum(x, 0.0) + jnp.log1p(jnp.exp(-jnp.abs(x))))
    cum = jnp.dot(decay, (row <= col).astype(F32), precision=HIGH, preferred_element_type=F32)
    beta = jax.nn.sigmoid(logits[0])
    for p in range(team):
        gates[p, pl.ds(0, hpm), :] = cum[p * hpm : (p + 1) * hpm]
        gates[p, pl.ds(hpm, hpm), :] = beta[p * hpm : (p + 1) * hpm]
    pl.semaphore_wait(barrier, len(away) + jnp.where(first, 0, 2))
    for who in away:
        remote(gates.at[who], seen.at[place], send_sem.at[GATES], recv_sem.at[GATES], {axis: base + who}).start()
    pltpu.make_async_copy(gates.at[place], seen.at[place], recv_sem.at[GATES]).start()
    spread(0)

    @pl.when(jnp.logical_not(first))
    def _():
        pl.semaphore_signal(rim_ready, inc=1, device_id={axis: base - 1}, device_id_type=MESH)
        pl.semaphore_signal(hop_ready, inc=1, device_id={axis: me - team}, device_id_type=MESH)

    spread(1)
    loaded(2)

    def rim(p, i):
        src, dst, width = streams[i]
        return remote(
            src.at[pl.ds(rows - RIM, RIM), pl.ds(p * width, width)], dst.at[pl.ds(0, RIM), :],
            rim_send.at[i], recv_sem.at[i], {axis: base + team + p},
        )

    @pl.when(feeds_rim)
    def _():
        pl.semaphore_wait(rim_ready, team)
        for i in range(len(streams)):
            for p in range(team):
                rim(p, i).start()

    @pl.when(first)
    def _():
        for _, dst, _ in streams:
            dst[pl.ds(0, RIM), :] = jnp.zeros((RIM, dst.shape[1]), BF)

    def arrived(ref, i):
        pltpu.make_async_copy(ref, ref, recv_sem.at[i]).wait()

    def stream(i):
        src, at, f_ref, count = plans[i]

        @pl.when(first)
        def _():
            arrived(src.at[pl.ds(RIM, team * rows), :], i)

        @pl.when(jnp.logical_not(first))
        def _():
            arrived(src, i)

        f_ref[...] = src[...].astype(F32)
        parts = []
        for b in range(team):
            for c in range(count):
                lanes = pl.ds(c * size, size)
                parts.append(
                    conv_silu(
                        lambda i: f_ref[pl.ds(RIM - taps + 1 + i + b * rows, rows), lanes], taps_s[at + c], rows
                    )
                )
        return parts

    arrived(seen, GATES)
    spread(2)
    cum_rows = jnp.concatenate([seen[b, pl.ds(0, hpm), :] for b in range(team)], axis=0)
    beta_rows = jnp.concatenate([seen[b, pl.ds(hpm, hpm), :] for b in range(team)], axis=0)
    pad = jnp.zeros((rows - 2 * units, rows), F32)
    columns = jnp.concatenate([cum_rows, beta_rows, pad], axis=0).T
    cum, beta = columns[:, :units], columns[:, units : 2 * units]
    growth = jnp.exp(cum)
    for u in range(units):
        ratio = jnp.exp(jnp.minimum(cum[:, u : u + 1] - cum_rows[u : u + 1], 0.0))
        r_s[u] = jnp.where(row >= col, ratio, 0.0)
    arrived(taps_s, TAPS)
    ks = stream(0)
    kn, kn_rows, ratios, inv = key_stage(ks, beta, [r_s[u] for u in range(units)], repeat)
    gain_rows = []
    for u in range(units):
        j = u // repeat
        r_s[u] = ratios[u]
        t_s[u] = inv[u].astype(BF)
        gain_rows.append(beta_rows[u : u + 1] * jnp.exp(cum_rows[u : u + 1]) * kn_rows[j : j + 1])
    drawn = [k.astype(F32).T for k in ks]
    ends = []
    for u in range(units):
        j = u // repeat
        tail_row = jnp.exp(cum_rows[u : u + 1, rows - 1 : rows] - cum_rows[u : u + 1])
        ends.append(mm(drawn[j] * (kn_rows[j : j + 1] * tail_row), t_s[u]))
        g_s[pl.ds(u, 1), :] = jnp.broadcast_to(growth[rows - 1 : rows, u : u + 1], (1, size))
    for u in range(units):
        m_s[u] = (-mm(ends[u] * gain_rows[u], ks[u // repeat])).astype(BF)
    ends = [(ends[u] * beta_rows[u : u + 1]).astype(BF) for u in range(units)]
    vs = stream(1)
    for u in range(units):
        b_s[u] = mm(ends[u], vs[u])

    def hop(h, to):
        return remote(sent.at[h], held.at[h], hop_send, hop_recv.at[h], {axis: to})

    def onward(h, state):
        @pl.when(jnp.logical_not(last))
        def _():
            sent[h] = state.astype(BF)
            if h == 0:
                pl.semaphore_wait(hop_ready, 1)
            hop(h, me + team).start()

    @pl.when(first)
    def _():
        states = [b_s[h] for h in range(hpm)]
        for h in range(hpm):
            s_s[h] = jnp.zeros((size, size), BF)
        for b in range(1, team):
            for h in range(hpm):
                u = b * hpm + h
                low = states[h].astype(BF)
                s_s[u] = low
                states[h] = (
                    b_s[u] + g_s[pl.ds(u, 1), :] * states[h] + jnp.dot(m_s[u], low, preferred_element_type=F32)
                )
        for h in range(hpm):
            onward(h, states[h])

    qs = stream(2)
    cross = [mm_nt(q, k) for q, k in zip(qs, ks)]
    qn = [norm(q) * size ** (-0.5) for q in qs]
    reads = [mm(r_s[u] * cross[u // repeat] * qn[u // repeat], t_s[u]) for u in range(units)]
    for u in range(units):
        j = u // repeat
        p_s[u] = (qs[j].astype(F32) * (qn[j] * growth[:, u : u + 1]) - mm(reads[u] * gain_rows[u], ks[j])).astype(BF)
        o_s[u] = mm(reads[u] * beta_rows[u : u + 1], vs[u])

    @pl.when(jnp.logical_not(first))
    def _():
        row, col = masks(size)
        eye = (row == col).astype(F32)
        turns = [g_s[pl.ds(h, 1), :] * eye + m_s[h].astype(F32) for h in range(hpm)]
        adds = [b_s[h] for h in range(hpm)]
        for b in range(1, team):
            for h in range(hpm):
                u = b * hpm + h
                low = jnp.concatenate([turns[h].astype(BF), adds[h].astype(BF)], axis=1)
                end = g_s[pl.ds(u, 1), :]
                moved = jnp.dot(m_s[u], low, preferred_element_type=F32)
                viewed = jnp.dot(p_s[u], low, preferred_element_type=F32)
                p_s[u] = viewed[:, :size].astype(BF)
                o_s[u] = o_s[u] + viewed[:, size:]
                turns[h] = end * turns[h] + moved[:, :size]
                adds[h] = b_s[u] + end * adds[h] + moved[:, size:]
        for h in range(hpm):
            m_s[h] = turns[h].astype(BF)
            b_s[h] = adds[h]

    pltpu.make_async_copy(gain_ref, gain, local_sem.at[2]).wait()
    ones = jnp.ones((2 * size, size), BF)
    for h in range(hpm):

        @pl.when(jnp.logical_not(first))
        def _():
            hop(h, me - team).wait_recv()

            @pl.when(jnp.logical_not(last))
            def _():
                onward(h, b_s[h] + jnp.dot(m_s[h], held[h], preferred_element_type=F32))

            for b in range(team):
                s_s[b * hpm + h] = held[h]

        mixed = [
            o_s[b * hpm + h] + jnp.dot(p_s[b * hpm + h], s_s[b * hpm + h], preferred_element_type=F32) for b in order
        ]
        squares = [x * x for x in mixed]
        heads_up = [x.astype(BF) for x in squares]
        rests = [(x - y.astype(F32)).astype(BF) for x, y in zip(squares, heads_up)]
        means = [mm(jnp.concatenate([x, y], axis=1), ones) * (1.0 / size) for x, y in zip(heads_up, rests)]
        for b, x, mean in zip(order, mixed, means):
            back[b, h] = (x * lax.rsqrt(mean + 1e-06) * gain[...]).astype(BF)
        lanes = pl.ds(pl.multiple_of(place * vw + h * size, size), size)
        for b in away:
            remote(back.at[b, h], out_ref.at[:, lanes], back_send, back_recv, {axis: base + b}).start()
        pltpu.make_async_copy(back.at[place, h], out_ref.at[:, lanes], back_recv).start()

    pltpu.make_async_copy(out_ref, out_ref, back_recv).wait()

    if away:
        gone(back.at[pl.ds(0, len(away))], back_send)
        gone(seen.at[pl.ds(0, len(away))], send_sem.at[GATES])
        for i in range(len(streams)):
            left(i)

    @pl.when(feeds_rim)
    def _():
        for i, (_, dst, _) in enumerate(streams):
            gone(dst.at[pl.ds(RIM, team * RIM), :], rim_send.at[i])

    @pl.when(jnp.logical_not(last))
    def _():
        gone(sent, hop_send)


def per_device(
    n, q_raw, k_raw, v_raw, gate_z, beta_logit, decay_in, conv_q, conv_k, conv_v, a_log, dt_bias, norm_gain
):
    size = norm_gain.shape[0]
    rows, width = q_raw.shape
    vwidth = v_raw.shape[1]
    heads = vwidth // size
    taps = conv_q.shape[0]
    team = math.gcd(n, width // size)
    kw, vw = width // team, vwidth // team
    kpm, hpm = kw // size, vw // size
    units = team * hpm
    long = RIM + team * rows
    grows = -(-2 * hpm // 8) * 8
    dma = pltpu.SemaphoreType.DMA
    normed = pl.pallas_call(
        functools.partial(mixer_kernel, "context", "tensor", n, team, size),
        out_shape=pltpu.VMEM((rows, vwidth), BF),
        in_specs=[pl.BlockSpec(memory_space=pltpu.HBM)] * 11,
        out_specs=pl.BlockSpec(memory_space=pltpu.VMEM),
        scratch_shapes=[
            pltpu.VMEM((rows, width), BF),
            pltpu.VMEM((rows, width), BF),
            pltpu.VMEM((rows, vwidth), BF),
            pltpu.VMEM((long, kw), BF),
            pltpu.VMEM((long, kw), BF),
            pltpu.VMEM((long, vw), BF),
            pltpu.VMEM((2, heads, rows), F32),
            pltpu.VMEM((team, grows, rows), F32),
            pltpu.VMEM((team, grows, rows), F32),
            pltpu.VMEM((2 * kpm + hpm, taps, size), BF),
            pltpu.VMEM((2, 1, heads), F32),
            pltpu.VMEM((1, size), F32),
            pltpu.VMEM((long, kw), F32),
            pltpu.VMEM((long, kw), F32),
            pltpu.VMEM((long, vw), F32),
            pltpu.VMEM((units, size, size), BF),
            pltpu.VMEM((units, size), F32),
            pltpu.VMEM((units, size, size), F32),
            pltpu.VMEM((units, rows, rows), F32),
            pltpu.VMEM((units, rows, rows), BF),
            pltpu.VMEM((units, size, size), BF),
            pltpu.VMEM((units, rows, size), BF),
            pltpu.VMEM((units, rows, size), F32),
            pltpu.VMEM((hpm, size, size), BF),
            pltpu.VMEM((hpm, size, size), BF),
            pltpu.VMEM((team, hpm, rows, size), BF),
            dma((6,)),
            dma((4,)),
            dma((5,)),
            dma((3,)),
            dma,
            dma((hpm,)),
            dma,
            dma,
            pltpu.SemaphoreType.REGULAR,
            pltpu.SemaphoreType.REGULAR,
        ],
        compiler_params=pltpu.CompilerParams(
            collective_id=0, has_side_effects=True, vmem_limit_bytes=60 << 20
        ),
        name="mixer",
    )(
        q_raw, k_raw, v_raw, beta_logit.T, decay_in.T, conv_q, conv_k, conv_v,
        a_log[None], dt_bias[None], norm_gain[None],
    )
    return (normed.astype(F32) * jax.nn.silu(gate_z.astype(F32))).astype(BF)


def solution(mesh):
    rows = P(("groups", "context"), "tensor")
    return jax.shard_map(
        functools.partial(per_device, mesh.shape["context"]),
        mesh=mesh,
        in_specs=(rows,) * 6 + (P(None, "tensor"),) * 3 + (P("tensor"),) * 2 + (P(),),
        out_specs=rows,
        check_vma=False,
    )
```

```python
import functools
import math

import jax
import jax.numpy as jnp
from jax import lax
from jax.experimental import pallas as pl
from jax.experimental.pallas import tpu as pltpu
from jax.sharding import PartitionSpec as P

MESH = pl.DeviceIdType.MESH
HIGH = lax.Precision.HIGHEST
RIM = 16
BF = jnp.bfloat16
F32 = jnp.float32


def mm(a, b):
    return jnp.dot(a.astype(BF), b.astype(BF), preferred_element_type=F32)


def mm_nt(a, b):
    return lax.dot_general(a.astype(BF), b.astype(BF), (((1,), (1,)), ((), ())), preferred_element_type=F32)


def conv_silu(full, weights, count):
    taps = weights.shape[0]
    total = weights[0:1].astype(F32) * full(0)
    for i in range(1, taps):
        total = total + weights[i : i + 1].astype(F32) * full(i)
    return (total * jax.nn.sigmoid(total)).astype(BF)


def norm(block):
    block = block.astype(F32)
    return 1.0 / jnp.sqrt(jnp.sum(block * block, axis=-1, keepdims=True) + 1e-06)


def masks(rows):
    row = lax.broadcasted_iota(jnp.int32, (rows, rows), 0)
    col = lax.broadcasted_iota(jnp.int32, (rows, rows), 1)
    return row, col


def halves(a, step):
    parts = [a[i : i + step] for i in range(0, a.shape[0], step)]
    return jnp.concatenate(parts[::2], axis=0), jnp.concatenate(parts[1::2], axis=0)


def less(a, change, step):
    if change.shape[0] == a.shape[0]:
        return a - change
    parts = []
    for i in range(0, a.shape[0], 2 * step):
        parts += [a[i : i + step], a[i + step : i + 2 * step] - change[i // 2 : i // 2 + step]]
    return jnp.concatenate(parts, axis=0)


def unit_scales(blocks):
    size = blocks[0].shape[1]
    down, along = jnp.ones((2 * size, blocks[0].shape[0]), BF), jnp.ones((8, 2 * size), BF)
    columns, lines = [], []
    for block in blocks:
        block = block.astype(F32)
        square = block * block
        high = square.astype(BF)
        both = jnp.concatenate([high, (square - high.astype(F32)).astype(BF)], axis=1)
        columns.append(lax.rsqrt(mm(both, down) + 1e-06))
        lines.append(lax.rsqrt(mm_nt(along, both)[:1] + 1e-06))
    return columns, lines


def key_stage(ks, weights, scales, repeat):
    rows = ks[0].shape[0]
    row, col = masks(rows)
    kn, kn_rows = unit_scales(ks)
    inner = [mm_nt(k, k) * c * r for k, c, r in zip(ks, kn, kn_rows)]
    lower = [weights[u] * inner[u // repeat] for u in range(weights.shape[0])]
    eye = (row == col).astype(F32)
    apart = row ^ col
    inv, rest = [], []
    for h, m in enumerate(lower):
        edge, full = jnp.where(apart == 1, m, 0.0), m + eye
        inv.append(((eye - edge) * scales[h : h + 1]).astype(BF))
        rest.append(full - mm(edge, full))
    step = 2
    while step < rows:
        mask = (apart >= step) & (apart < 2 * step)
        for h in range(len(lower)):
            edge = jnp.where(mask, rest[h], 0.0)
            if step >= 16:
                edge = halves(edge, step)[1]
            if 2 * step < rows:
                both = mm(edge, jnp.concatenate([inv[h], rest[h].astype(BF)], axis=1))
                inv[h], rest[h] = less(inv[h], both[:, :rows].astype(BF), step), less(rest[h], both[:, rows:], step)
            else:
                inv[h] = less(inv[h], mm(edge, inv[h]).astype(BF), step)
        step *= 2
    return kn_rows, inv


def mixer_kernel(
    axis, side, n, team, size,
    q_ref, k_ref, v_ref, bl_ref, di_ref, wq_ref, wk_ref, wv_ref, al_ref, dt_ref, gain_ref, gate_ref,
    out_ref,
    gate_own, gate_s, got,    q_own, k_own, v_own, q_rows, k_rows, v_rows, logits, gates, seen, taps_s, scales, gain,
    fq, fk, fv, m_s, g_s, b_s, r_s, l_s, t_s, s_s, p_s, o_s, held, sent, back,
    local_sem, send_sem, recv_sem, rim_send, hop_send, hop_recv, back_send, back_recv, rim_ready, hop_ready,
):
    me = lax.axis_index(axis)
    place, turn = lax.rem(me, team), me // team
    base = turn * team
    rows = q_ref.shape[0]
    taps = wq_ref.shape[0]
    kw, vw = wq_ref.shape[1] // team, wv_ref.shape[1] // team
    kpm, hpm = kw // size, vw // size
    repeat = hpm // kpm
    units = team * hpm
    first, last = turn == 0, turn == n // team - 1
    tail_place = place == team - 1
    feeds_rim = tail_place & jnp.logical_not(last)
    streams = ((k_own, k_rows, kw), (v_own, v_rows, vw), (q_own, q_rows, kw))
    plans = ((k_rows, 0, fk, kpm), (v_rows, kpm, fv, hpm), (q_rows, kpm + hpm, fq, kpm))
    GATES, TAPS = 3, 4
    core = lax.axis_index(side)
    if team == 4:
        order = [3 - place, lax.rem(place + 2, team), place + 1 - 2 * lax.rem(place, 2), place]
    else:
        order = [lax.rem(place + d, team) for d in range(1, team)] + [place]
    away = order[:-1]

    def lanes_of(who, width):
        return pl.ds(pl.multiple_of(who * width, width), width)

    def rows_of(who):
        return pl.ds(pl.multiple_of(RIM + who * rows, RIM), rows)

    def remote(src, dst, send, recv, to):
        return pltpu.make_async_remote_copy(
            src_ref=src, dst_ref=dst, send_sem=send, recv_sem=recv, device_id=to, device_id_type=MESH
        )

    def loaded(i):
        pltpu.make_async_copy(streams[i][0], streams[i][0], local_sem.at[3 + i]).wait()

    def spread(i):
        src, dst, width = streams[i]
        if i < 2:
            loaded(i)
        for who in away:
            remote(
                src.at[:, lanes_of(who, width)], dst.at[rows_of(place), :],
                send_sem.at[i], recv_sem.at[i], {axis: base + who},
            ).start()
        pltpu.make_async_copy(src.at[:, lanes_of(place, width)], dst.at[rows_of(place), :], recv_sem.at[i]).start()

    def gone(ref, sem):
        pltpu.make_async_copy(ref, ref, sem).wait()

    def left(i):
        gone(streams[i][1].at[pl.ds(RIM, len(away) * rows), :], send_sem.at[i])

    def tap_pieces():
        pieces = []
        at = 0
        for ref, count in ((wk_ref, kpm), (wv_ref, hpm), (wq_ref, kpm)):
            for c in range(count):
                lanes = pl.ds(pl.multiple_of((place * count + c) * size, size), size)
                pieces.append((ref.at[:, lanes], taps_s.at[at]))
                at += 1
        return pieces

    loads = [
        (bl_ref, logits.at[0], 0), (di_ref, logits.at[1], 0), (al_ref, scales.at[0], 1), (dt_ref, scales.at[1], 1),
        (gain_ref, gain, 2), (k_ref, k_own, 3), (v_ref, v_own, 4), (q_ref, q_own, 5),
        (gate_ref, gate_own, 6),
    ]
    barrier = pltpu.get_barrier_semaphore()

    def greet(to):
        pl.semaphore_signal(barrier, inc=1, device_id=to, device_id_type=MESH)

    for who in away:
        greet({axis: base + who})

    @pl.when(jnp.logical_not(last))
    def _():
        greet({axis: me + team})

    @pl.when(feeds_rim)
    def _():
        for p in range(team):
            greet({axis: base + team + p})

    for src, dst, i in loads:
        pltpu.make_async_copy(src, dst, local_sem.at[i]).start()
    for src, dst in tap_pieces():
        pltpu.make_async_copy(src, dst, recv_sem.at[TAPS]).start()

    pltpu.make_async_copy(logits, logits, local_sem.at[0]).wait()
    pltpu.make_async_copy(scales, scales, local_sem.at[1]).wait()
    heads = bl_ref.shape[0]
    diag = lax.broadcasted_iota(jnp.int32, (heads, heads), 0) == lax.broadcasted_iota(jnp.int32, (heads, heads), 1)

    def upright(row):
        return jnp.sum(jnp.where(diag, row, 0.0), axis=1, keepdims=True)

    row, col = masks(rows)
    x = logits[1] + upright(scales[1])
    decay = -jnp.exp(upright(scales[0])) * (jnp.maximum(x, 0.0) + jnp.log1p(jnp.exp(-jnp.abs(x))))
    cum = jnp.dot(decay, (row <= col).astype(F32), precision=HIGH, preferred_element_type=F32)
    beta = jax.nn.sigmoid(logits[0])
    for p in range(team):
        gates[p, pl.ds(0, hpm), :] = cum[p * hpm : (p + 1) * hpm]
        gates[p, pl.ds(hpm, hpm), :] = beta[p * hpm : (p + 1) * hpm]
    pl.semaphore_wait(barrier, len(away) + jnp.where(first, 0, 2))

    @pl.when(jnp.logical_not(first))
    def _():
        pl.semaphore_signal(rim_ready, inc=1, device_id={axis: base - 1}, device_id_type=MESH)
        pl.semaphore_signal(hop_ready, inc=1, device_id={axis: me - team}, device_id_type=MESH)

    for who in away:
        remote(gates.at[who], seen.at[place], send_sem.at[GATES], recv_sem.at[GATES], {axis: base + who}).start()
    pltpu.make_async_copy(gates.at[place], seen.at[place], recv_sem.at[GATES]).start()
    spread(0)

    spread(1)
    loaded(2)
    pltpu.make_async_copy(gate_own, gate_own, local_sem.at[6]).wait()
    gate_s[...] = jax.nn.silu(gate_own[...].astype(F32))

    def rim(p, i):
        src, dst, width = streams[i]
        return remote(
            src.at[pl.ds(rows - RIM, RIM), pl.ds(p * width, width)], dst.at[pl.ds(0, RIM), :],
            rim_send.at[i], recv_sem.at[i], {axis: base + team + p},
        )

    @pl.when(feeds_rim)
    def _():
        pl.semaphore_wait(rim_ready, team)
        for i in range(len(streams)):
            for p in range(team):
                rim(p, i).start()

    @pl.when(first)
    def _():
        for _, dst, _ in streams:
            dst[pl.ds(0, RIM), :] = jnp.zeros((RIM, dst.shape[1]), BF)

    def arrived(ref, i):
        pltpu.make_async_copy(ref, ref, recv_sem.at[i]).wait()

    def stream(i):
        src, at, f_ref, count = plans[i]

        @pl.when(first)
        def _():
            arrived(src.at[pl.ds(RIM, team * rows), :], i)

        @pl.when(jnp.logical_not(first))
        def _():
            arrived(src, i)

        f_ref[...] = src[...].astype(F32)
        parts = []
        for b in range(team):
            for c in range(count):
                lanes = pl.ds(c * size, size)
                parts.append(
                    conv_silu(
                        lambda i: f_ref[pl.ds(RIM - taps + 1 + i + b * rows, rows), lanes], taps_s[at + c], rows
                    )
                )
        return parts

    arrived(seen, GATES)
    pl.when((core == 0) | jnp.logical_not(first))(functools.partial(spread, 2))
    cum_rows = jnp.concatenate([seen[b, pl.ds(0, hpm), :] for b in range(team)], axis=0)
    beta_rows = jnp.concatenate([seen[b, pl.ds(hpm, hpm), :] for b in range(team)], axis=0)
    pad = jnp.zeros((rows - 2 * units, rows), F32)
    columns = jnp.concatenate([cum_rows, beta_rows, pad], axis=0).T
    cum, beta = columns[:, :units], columns[:, units : 2 * units]
    growth = jnp.exp(cum)
    for u in range(units):
        ratio = jnp.exp(jnp.minimum(cum[:, u : u + 1] - cum_rows[u : u + 1], 0.0))
        r_s[u] = jnp.where(row >= col, ratio, 0.0)
        l_s[u] = jnp.where(row > col, ratio * beta[:, u : u + 1], 0.0)
    arrived(taps_s, TAPS)
    ks = stream(0)
    kn_rows, inv = key_stage(ks, l_s, beta_rows, repeat)
    pl.when((core == 1) & first)(functools.partial(spread, 2))
    gain_rows = []
    for u in range(units):
        j = u // repeat
        t_s[u] = inv[u]
        gain_rows.append(jnp.exp(cum_rows[u : u + 1]) * kn_rows[j])
    drawn = [k.astype(F32).T for k in ks]
    ends = []
    for u in range(units):
        j = u // repeat
        tail_row = jnp.exp(cum_rows[u : u + 1, rows - 1 : rows] - cum_rows[u : u + 1])
        ends.append(mm(drawn[j] * (kn_rows[j] * tail_row), t_s[u]))
        g_s[pl.ds(u, 1), :] = jnp.broadcast_to(growth[rows - 1 : rows, u : u + 1], (1, size))
    for u in range(units):
        m_s[u] = (-mm(ends[u] * gain_rows[u], ks[u // repeat])).astype(BF)
    ends = [end.astype(BF) for end in ends]
    vs = stream(1)
    for u in range(units):
        b_s[u] = mm(ends[u], vs[u])

    def hop(h, to):
        return remote(sent.at[h], held.at[h], hop_send, hop_recv.at[h], {axis: to})

    def onward(h, state):
        @pl.when(jnp.logical_not(last))
        def _():
            sent[h] = state.astype(BF)
            if h == 0:
                pl.semaphore_wait(hop_ready, 1)
            hop(h, me + team).start()

    @pl.when(first)
    def _():
        states = [b_s[h] for h in range(hpm)]
        for h in range(hpm):
            s_s[h] = jnp.zeros((size, size), BF)
        for b in range(1, team):
            for h in range(hpm):
                u = b * hpm + h
                low = states[h].astype(BF)
                s_s[u] = low
                states[h] = (
                    b_s[u] + g_s[pl.ds(u, 1), :] * states[h] + jnp.dot(m_s[u], low, preferred_element_type=F32)
                )
        for h in range(hpm):
            onward(h, states[h])

    qs = stream(2)
    qn = [norm(q) * size ** (-0.5) for q in qs]
    cross = [mm_nt(q, k) * c * r for q, k, c, r in zip(qs, ks, qn, kn_rows)]
    reads = [mm(r_s[u] * cross[u // repeat], t_s[u]) for u in range(units)]
    for u in range(units):
        j = u // repeat
        p_s[u] = (qs[j].astype(F32) * (qn[j] * growth[:, u : u + 1]) - mm(reads[u] * gain_rows[u], ks[j])).astype(BF)
        o_s[u] = mm(reads[u], vs[u])

    @pl.when(jnp.logical_not(first))
    def _():
        row, col = masks(size)
        eye = (row == col).astype(F32)
        turns = [g_s[pl.ds(h, 1), :] * eye + m_s[h].astype(F32) for h in range(hpm)]
        adds = [b_s[h] for h in range(hpm)]
        for b in range(1, team):
            for h in range(hpm):
                u = b * hpm + h
                low = jnp.concatenate([turns[h].astype(BF), adds[h].astype(BF)], axis=1)
                end = g_s[pl.ds(u, 1), :]
                moved = jnp.dot(m_s[u], low, preferred_element_type=F32)
                viewed = jnp.dot(p_s[u], low, preferred_element_type=F32)
                p_s[u] = viewed[:, :size].astype(BF)
                o_s[u] = o_s[u] + viewed[:, size:]
                turns[h] = end * turns[h] + moved[:, :size]
                adds[h] = b_s[u] + end * adds[h] + moved[:, size:]
        for h in range(hpm):
            m_s[h] = turns[h].astype(BF)
            b_s[h] = adds[h]

    pltpu.make_async_copy(gain_ref, gain, local_sem.at[2]).wait()
    ones = jnp.ones((2 * size, size), BF)
    def finish(pairs):
        mixed = [
            o_s[b * hpm + h] + jnp.dot(p_s[b * hpm + h], s_s[b * hpm + h], preferred_element_type=F32)
            for b, h in pairs
        ]
        squares = [x * x for x in mixed]
        heads_up = [x.astype(BF) for x in squares]
        rests = [(x - y.astype(F32)).astype(BF) for x, y in zip(squares, heads_up)]
        means = [mm(jnp.concatenate([x, y], axis=1), ones) * (1.0 / size) for x, y in zip(heads_up, rests)]
        for (b, h), x, mean in zip(pairs, mixed, means):
            back[b, h] = (x * lax.rsqrt(mean + 1e-06) * gain[...]).astype(BF)

    def lanes_at(h):
        return pl.ds(pl.multiple_of(place * vw + h * size, size), size)

    for h in range(hpm):

        @pl.when(jnp.logical_not(first))
        def _():
            hop(h, me - team).wait_recv()

            @pl.when(jnp.logical_not(last))
            def _():
                onward(h, b_s[h] + jnp.dot(m_s[h], held[h], preferred_element_type=F32))

            for b in range(team):
                s_s[b * hpm + h] = held[h]

        if away:
            finish([(b, h) for b in away])
        for b in away:
            remote(back.at[b, h], got.at[:, lanes_at(h)], back_send, back_recv, {axis: base + b}).start()

    finish([(place, h) for h in range(hpm)])
    for h in range(hpm):
        pltpu.make_async_copy(back.at[place, h], got.at[:, lanes_at(h)], back_recv).start()

    pltpu.make_async_copy(got, got, back_recv).wait()
    out_ref[...] = (got[...].astype(F32) * gate_s[...]).astype(BF)

    if away:
        gone(back.at[pl.ds(0, len(away))], back_send)
        gone(seen.at[pl.ds(0, len(away))], send_sem.at[GATES])
        for i in range(len(streams)):
            left(i)

    @pl.when(feeds_rim)
    def _():
        for i, (_, dst, _) in enumerate(streams):
            gone(dst.at[pl.ds(RIM, team * RIM), :], rim_send.at[i])

    @pl.when(jnp.logical_not(last))
    def _():
        gone(sent, hop_send)


def per_device(
    n, q_raw, k_raw, v_raw, gate_z, beta_logit, decay_in, conv_q, conv_k, conv_v, a_log, dt_bias, norm_gain
):
    size = norm_gain.shape[0]
    rows, width = q_raw.shape
    vwidth = v_raw.shape[1]
    heads = vwidth // size
    taps = conv_q.shape[0]
    team = math.gcd(n, width // size)
    kw, vw = width // team, vwidth // team
    kpm, hpm = kw // size, vw // size
    units = team * hpm
    long = RIM + team * rows
    grows = -(-2 * hpm // 8) * 8
    dma = pltpu.SemaphoreType.DMA
    return pl.pallas_call(
        functools.partial(mixer_kernel, "context", "tensor", n, team, size),
        out_shape=pltpu.VMEM((rows, vwidth), BF),
        in_specs=[pl.BlockSpec(memory_space=pltpu.HBM)] * 12,
        out_specs=pl.BlockSpec(memory_space=pltpu.VMEM),
        scratch_shapes=[
            pltpu.VMEM((rows, vwidth), BF),
            pltpu.VMEM((rows, vwidth), F32),
            pltpu.VMEM((rows, vwidth), BF),
            pltpu.VMEM((rows, width), BF),
            pltpu.VMEM((rows, width), BF),
            pltpu.VMEM((rows, vwidth), BF),
            pltpu.VMEM((long, kw), BF),
            pltpu.VMEM((long, kw), BF),
            pltpu.VMEM((long, vw), BF),
            pltpu.VMEM((2, heads, rows), F32),
            pltpu.VMEM((team, grows, rows), F32),
            pltpu.VMEM((team, grows, rows), F32),
            pltpu.VMEM((2 * kpm + hpm, taps, size), BF),
            pltpu.VMEM((2, 1, heads), F32),
            pltpu.VMEM((1, size), F32),
            pltpu.VMEM((long, kw), F32),
            pltpu.VMEM((long, kw), F32),
            pltpu.VMEM((long, vw), F32),
            pltpu.VMEM((units, size, size), BF),
            pltpu.VMEM((units, size), F32),
            pltpu.VMEM((units, size, size), F32),
            pltpu.VMEM((units, rows, rows), F32),
            pltpu.VMEM((units, rows, rows), F32),
            pltpu.VMEM((units, rows, rows), BF),
            pltpu.VMEM((units, size, size), BF),
            pltpu.VMEM((units, rows, size), BF),
            pltpu.VMEM((units, rows, size), F32),
            pltpu.VMEM((hpm, size, size), BF),
            pltpu.VMEM((hpm, size, size), BF),
            pltpu.VMEM((team, hpm, rows, size), BF),
            dma((7,)),
            dma((4,)),
            dma((5,)),
            dma((3,)),
            dma,
            dma((hpm,)),
            dma,
            dma,
            pltpu.SemaphoreType.REGULAR,
            pltpu.SemaphoreType.REGULAR,
        ],
        compiler_params=pltpu.CompilerParams(
            collective_id=0, has_side_effects=True, vmem_limit_bytes=60 << 20
        ),
        name="mixer",
    )(
        q_raw, k_raw, v_raw, beta_logit.T, decay_in.T, conv_q, conv_k, conv_v,
        a_log[None], dt_bias[None], norm_gain[None], gate_z,
    )


def solution(mesh):
    rows = P(("groups", "context"), "tensor")
    return jax.shard_map(
        functools.partial(per_device, mesh.shape["context"]),
        mesh=mesh,
        in_specs=(rows,) * 6 + (P(None, "tensor"),) * 3 + (P("tensor"),) * 2 + (P(),),
        out_specs=rows,
        check_vma=False,
    )
```

```python
import functools
import math

import jax
import jax.numpy as jnp
from jax import lax
from jax.experimental import pallas as pl
from jax.experimental.pallas import tpu as pltpu
from jax.sharding import PartitionSpec as P

MESH = pl.DeviceIdType.MESH
HIGH = lax.Precision.HIGHEST
RIM = 16
BF = jnp.bfloat16
F32 = jnp.float32


def mm(a, b):
    return jnp.dot(a.astype(BF), b.astype(BF), preferred_element_type=F32)


def mm_nt(a, b):
    return lax.dot_general(a.astype(BF), b.astype(BF), (((1,), (1,)), ((), ())), preferred_element_type=F32)


def conv_silu(full, weights, count):
    taps = weights.shape[0]
    total = weights[0:1].astype(F32) * full(0)
    for i in range(1, taps):
        total = total + weights[i : i + 1].astype(F32) * full(i)
    return (total * jax.nn.sigmoid(total)).astype(BF)


def norm(block):
    block = block.astype(F32)
    return 1.0 / jnp.sqrt(jnp.sum(block * block, axis=-1, keepdims=True) + 1e-06)


def masks(rows):
    row = lax.broadcasted_iota(jnp.int32, (rows, rows), 0)
    col = lax.broadcasted_iota(jnp.int32, (rows, rows), 1)
    return row, col


def halves(a, step):
    parts = [a[i : i + step] for i in range(0, a.shape[0], step)]
    return jnp.concatenate(parts[::2], axis=0), jnp.concatenate(parts[1::2], axis=0)


def less(a, change, step):
    if change.shape[0] == a.shape[0]:
        return a - change
    parts = []
    for i in range(0, a.shape[0], 2 * step):
        parts += [a[i : i + step], a[i + step : i + 2 * step] - change[i // 2 : i // 2 + step]]
    return jnp.concatenate(parts, axis=0)


def unit_scales(blocks):
    size = blocks[0].shape[1]
    down, along = jnp.ones((2 * size, blocks[0].shape[0]), BF), jnp.ones((8, 2 * size), BF)
    columns, lines = [], []
    for block in blocks:
        block = block.astype(F32)
        square = block * block
        high = square.astype(BF)
        both = jnp.concatenate([high, (square - high.astype(F32)).astype(BF)], axis=1)
        columns.append(lax.rsqrt(mm(both, down) + 1e-06))
        lines.append(lax.rsqrt(mm_nt(along, both)[:1] + 1e-06))
    return columns, lines


def key_stage(ks, weights, scales, repeat):
    rows = ks[0].shape[0]
    row, col = masks(rows)
    kn, kn_rows = unit_scales(ks)
    inner = [mm_nt(k, k) * c * r for k, c, r in zip(ks, kn, kn_rows)]
    lower = [weights[u] * inner[u // repeat] for u in range(weights.shape[0])]
    eye = (row == col).astype(F32)
    apart = row ^ col
    inv, rest = [], []
    for h, m in enumerate(lower):
        edge, full = jnp.where(apart == 1, m, 0.0), m + eye
        inv.append(((eye - edge) * scales[h : h + 1]).astype(BF))
        rest.append(full - mm(edge, full))
    step = 2
    while step < rows:
        mask = (apart >= step) & (apart < 2 * step)
        for h in range(len(lower)):
            edge = jnp.where(mask, rest[h], 0.0)
            if step >= 16:
                edge = halves(edge, step)[1]
            if 2 * step < rows:
                both = mm(edge, jnp.concatenate([inv[h], rest[h].astype(BF)], axis=1))
                inv[h], rest[h] = less(inv[h], both[:, :rows].astype(BF), step), less(rest[h], both[:, rows:], step)
            else:
                inv[h] = less(inv[h], mm(edge, inv[h]).astype(BF), step)
        step *= 2
    return kn_rows, inv


def mixer_kernel(
    axis, side, n, team, size,
    q_ref, k_ref, v_ref, bl_ref, di_ref, wq_ref, wk_ref, wv_ref, al_ref, dt_ref, gain_ref, gate_ref,
    out_ref,
    gate_own, gate_s, got,    q_own, k_own, v_own, q_rows, k_rows, v_rows, logits, gates, seen, taps_s, scales, gain,
    fq, fk, fv, m_s, g_s, b_s, r_s, l_s, t_s, s_s, p_s, o_s, held, sent, back,
    local_sem, send_sem, recv_sem, hop_recv, back_send, back_recv, rim_ready, hop_ready,
):
    me = lax.axis_index(axis)
    place, turn = lax.rem(me, team), me // team
    base = turn * team
    rows = q_ref.shape[0]
    taps = wq_ref.shape[0]
    kw, vw = wq_ref.shape[1] // team, wv_ref.shape[1] // team
    kpm, hpm = kw // size, vw // size
    repeat = hpm // kpm
    units = team * hpm
    first, last = turn == 0, turn == n // team - 1
    tail_place = place == team - 1
    feeds_rim = tail_place & jnp.logical_not(last)
    streams = ((k_own, k_rows, kw), (v_own, v_rows, vw), (q_own, q_rows, kw))
    plans = ((k_rows, 0, fk, kpm), (v_rows, kpm, fv, hpm), (q_rows, kpm + hpm, fq, kpm))
    GATES, TAPS = 3, 4
    core = lax.axis_index(side)
    if team == 4:
        order = [3 - place, lax.rem(place + 2, team), place + 1 - 2 * lax.rem(place, 2), place]
    else:
        order = [lax.rem(place + d, team) for d in range(1, team)] + [place]
    away = order[:-1]

    def lanes_of(who, width):
        return pl.ds(pl.multiple_of(who * width, width), width)

    def rows_of(who):
        return pl.ds(pl.multiple_of(RIM + who * rows, RIM), rows)

    def remote(src, dst, send, recv, to):
        return pltpu.make_async_remote_copy(
            src_ref=src, dst_ref=dst, send_sem=send, recv_sem=recv, device_id=to, device_id_type=MESH
        )

    def loaded(i):
        pltpu.make_async_copy(streams[i][0], streams[i][0], local_sem.at[3 + i]).wait()

    def spread(i):
        src, dst, width = streams[i]
        if i < 2:
            loaded(i)
        for who in away:
            remote(
                src.at[:, lanes_of(who, width)], dst.at[rows_of(place), :],
                send_sem.at[i], recv_sem.at[i], {axis: base + who},
            ).start()
        pltpu.make_async_copy(src.at[:, lanes_of(place, width)], dst.at[rows_of(place), :], recv_sem.at[i]).start()

    def gone(ref, sem):
        pltpu.make_async_copy(ref, ref, sem).wait()

    def tap_pieces():
        pieces = []
        at = 0
        for ref, count in ((wk_ref, kpm), (wv_ref, hpm), (wq_ref, kpm)):
            for c in range(count):
                lanes = pl.ds(pl.multiple_of((place * count + c) * size, size), size)
                pieces.append((ref.at[:, lanes], taps_s.at[at]))
                at += 1
        return pieces

    loads = [
        (bl_ref, logits.at[0], 0), (di_ref, logits.at[1], 0), (al_ref, scales.at[0], 1), (dt_ref, scales.at[1], 1),
        (gain_ref, gain, 2), (k_ref, k_own, 3), (v_ref, v_own, 4), (q_ref, q_own, 5),
        (gate_ref, gate_own, 6),
    ]
    barrier = pltpu.get_barrier_semaphore()

    def greet(to):
        pl.semaphore_signal(barrier, inc=1, device_id=to, device_id_type=MESH)

    for who in away:
        greet({axis: base + who})

    @pl.when(jnp.logical_not(last))
    def _():
        greet({axis: me + team})

    @pl.when(feeds_rim)
    def _():
        for p in range(team):
            greet({axis: base + team + p})

    for src, dst, i in loads:
        pltpu.make_async_copy(src, dst, local_sem.at[i]).start()
    for src, dst in tap_pieces():
        pltpu.make_async_copy(src, dst, recv_sem.at[TAPS]).start()

    pltpu.make_async_copy(logits, logits, local_sem.at[0]).wait()
    pltpu.make_async_copy(scales, scales, local_sem.at[1]).wait()
    heads = bl_ref.shape[0]
    diag = lax.broadcasted_iota(jnp.int32, (heads, heads), 0) == lax.broadcasted_iota(jnp.int32, (heads, heads), 1)

    def upright(row):
        return jnp.sum(jnp.where(diag, row, 0.0), axis=1, keepdims=True)

    row, col = masks(rows)
    x = logits[1] + upright(scales[1])
    decay = -jnp.exp(upright(scales[0])) * (jnp.maximum(x, 0.0) + jnp.log1p(jnp.exp(-jnp.abs(x))))
    cum = jnp.dot(decay, (row <= col).astype(F32), precision=HIGH, preferred_element_type=F32)
    beta = jax.nn.sigmoid(logits[0])
    for p in range(team):
        gates[p, pl.ds(0, hpm), :] = cum[p * hpm : (p + 1) * hpm]
        gates[p, pl.ds(hpm, hpm), :] = beta[p * hpm : (p + 1) * hpm]
    pl.semaphore_wait(barrier, len(away) + jnp.where(first, 0, 2))

    @pl.when(jnp.logical_not(first))
    def _():
        pl.semaphore_signal(rim_ready, inc=1, device_id={axis: base - 1}, device_id_type=MESH)
        pl.semaphore_signal(hop_ready, inc=1, device_id={axis: me - team}, device_id_type=MESH)

    for who in away:
        remote(gates.at[who], seen.at[place], send_sem.at[GATES], recv_sem.at[GATES], {axis: base + who}).start()
    pltpu.make_async_copy(gates.at[place], seen.at[place], recv_sem.at[GATES]).start()
    spread(0)

    spread(1)
    loaded(2)
    pltpu.make_async_copy(gate_own, gate_own, local_sem.at[6]).wait()
    gate_s[...] = jax.nn.silu(gate_own[...].astype(F32))

    def rim(p, i):
        src, dst, width = streams[i]
        return remote(
            src.at[pl.ds(rows - RIM, RIM), pl.ds(p * width, width)], dst.at[pl.ds(0, RIM), :],
            send_sem.at[i], recv_sem.at[i], {axis: base + team + p},
        )

    @pl.when(feeds_rim)
    def _():
        pl.semaphore_wait(rim_ready, team)
        for i in range(len(streams)):
            for p in range(team):
                rim(p, i).start()

    @pl.when(first)
    def _():
        for _, dst, _ in streams:
            dst[pl.ds(0, RIM), :] = jnp.zeros((RIM, dst.shape[1]), BF)

    def arrived(ref, i):
        pltpu.make_async_copy(ref, ref, recv_sem.at[i]).wait()

    def stream(i):
        src, at, f_ref, count = plans[i]

        @pl.when(first)
        def _():
            arrived(src.at[pl.ds(RIM, team * rows), :], i)

        @pl.when(jnp.logical_not(first))
        def _():
            arrived(src, i)

        f_ref[...] = src[...].astype(F32)
        parts = []
        for b in range(team):
            for c in range(count):
                lanes = pl.ds(c * size, size)
                parts.append(
                    conv_silu(
                        lambda i: f_ref[pl.ds(RIM - taps + 1 + i + b * rows, rows), lanes], taps_s[at + c], rows
                    )
                )
        return parts

    arrived(seen, GATES)
    pl.when((core == 0) | jnp.logical_not(first))(functools.partial(spread, 2))
    cum_rows = jnp.concatenate([seen[b, pl.ds(0, hpm), :] for b in range(team)], axis=0)
    beta_rows = jnp.concatenate([seen[b, pl.ds(hpm, hpm), :] for b in range(team)], axis=0)
    pad = jnp.zeros((rows - 2 * units, rows), F32)
    columns = jnp.concatenate([cum_rows, beta_rows, pad], axis=0).T
    cum, beta = columns[:, :units], columns[:, units : 2 * units]
    growth = jnp.exp(cum)
    for u in range(units):
        ratio = jnp.exp(jnp.minimum(cum[:, u : u + 1] - cum_rows[u : u + 1], 0.0))
        r_s[u] = jnp.where(row >= col, ratio, 0.0)
        l_s[u] = jnp.where(row > col, ratio * beta[:, u : u + 1], 0.0)
    arrived(taps_s, TAPS)
    ks = stream(0)
    kn_rows, inv = key_stage(ks, l_s, beta_rows, repeat)
    pl.when((core == 1) & first)(functools.partial(spread, 2))
    gain_rows = []
    for u in range(units):
        j = u // repeat
        t_s[u] = inv[u]
        gain_rows.append(jnp.exp(cum_rows[u : u + 1]) * kn_rows[j])
    drawn = [k.astype(F32).T for k in ks]
    ends = []
    for u in range(units):
        j = u // repeat
        tail_row = jnp.exp(cum_rows[u : u + 1, rows - 1 : rows] - cum_rows[u : u + 1])
        ends.append(mm(drawn[j] * (kn_rows[j] * tail_row), t_s[u]))
        g_s[pl.ds(u, 1), :] = jnp.broadcast_to(growth[rows - 1 : rows, u : u + 1], (1, size))
    for u in range(units):
        m_s[u] = (-mm(ends[u] * gain_rows[u], ks[u // repeat])).astype(BF)
    ends = [end.astype(BF) for end in ends]
    vs = stream(1)
    for u in range(units):
        b_s[u] = mm(ends[u], vs[u])

    def hop(h, to):
        return remote(sent.at[h], held.at[h], back_send, hop_recv.at[h], {axis: to})

    def onward(h, state):
        @pl.when(jnp.logical_not(last))
        def _():
            sent[h] = state.astype(BF)
            if h == 0:
                pl.semaphore_wait(hop_ready, 1)
            hop(h, me + team).start()

    @pl.when(first)
    def _():
        states = [b_s[h] for h in range(hpm)]
        for h in range(hpm):
            s_s[h] = jnp.zeros((size, size), BF)
        for b in range(1, team):
            for h in range(hpm):
                u = b * hpm + h
                low = states[h].astype(BF)
                s_s[u] = low
                states[h] = (
                    b_s[u] + g_s[pl.ds(u, 1), :] * states[h] + jnp.dot(m_s[u], low, preferred_element_type=F32)
                )
        for h in range(hpm):
            onward(h, states[h])

    qs = stream(2)
    qn = [norm(q) * size ** (-0.5) for q in qs]
    cross = [mm_nt(q, k) * c * r for q, k, c, r in zip(qs, ks, qn, kn_rows)]
    reads = [mm(r_s[u] * cross[u // repeat], t_s[u]) for u in range(units)]
    for u in range(units):
        j = u // repeat
        p_s[u] = (qs[j].astype(F32) * (qn[j] * growth[:, u : u + 1]) - mm(reads[u] * gain_rows[u], ks[j])).astype(BF)
        o_s[u] = mm(reads[u], vs[u])

    @pl.when(jnp.logical_not(first))
    def _():
        row, col = masks(size)
        eye = (row == col).astype(F32)
        turns = [g_s[pl.ds(h, 1), :] * eye + m_s[h].astype(F32) for h in range(hpm)]
        adds = [b_s[h] for h in range(hpm)]
        for b in range(1, team):
            for h in range(hpm):
                u = b * hpm + h
                low = jnp.concatenate([turns[h].astype(BF), adds[h].astype(BF)], axis=1)
                end = g_s[pl.ds(u, 1), :]
                moved = jnp.dot(m_s[u], low, preferred_element_type=F32)
                viewed = jnp.dot(p_s[u], low, preferred_element_type=F32)
                p_s[u] = viewed[:, :size].astype(BF)
                o_s[u] = o_s[u] + viewed[:, size:]
                turns[h] = end * turns[h] + moved[:, :size]
                adds[h] = b_s[u] + end * adds[h] + moved[:, size:]
        for h in range(hpm):
            m_s[h] = turns[h].astype(BF)
            b_s[h] = adds[h]

    pltpu.make_async_copy(gain_ref, gain, local_sem.at[2]).wait()
    ones = jnp.ones((2 * size, size), BF)
    def finish(pairs):
        mixed = [
            o_s[b * hpm + h] + jnp.dot(p_s[b * hpm + h], s_s[b * hpm + h], preferred_element_type=F32)
            for b, h in pairs
        ]
        squares = [x * x for x in mixed]
        heads_up = [x.astype(BF) for x in squares]
        rests = [(x - y.astype(F32)).astype(BF) for x, y in zip(squares, heads_up)]
        means = [mm(jnp.concatenate([x, y], axis=1), ones) * (1.0 / size) for x, y in zip(heads_up, rests)]
        for (b, h), x, mean in zip(pairs, mixed, means):
            back[b, h] = (x * lax.rsqrt(mean + 1e-06) * gain[...]).astype(BF)

    def lanes_at(h):
        return pl.ds(pl.multiple_of(place * vw + h * size, size), size)

    for h in range(hpm):

        @pl.when(jnp.logical_not(first))
        def _():
            hop(h, me - team).wait_recv()

            @pl.when(jnp.logical_not(last))
            def _():
                onward(h, b_s[h] + jnp.dot(m_s[h], held[h], preferred_element_type=F32))

            for b in range(team):
                s_s[b * hpm + h] = held[h]

        if away:
            finish([(b, h) for b in away])
        for b in away:
            remote(back.at[b, h], got.at[:, lanes_at(h)], back_send, back_recv, {axis: base + b}).start()

    finish([(place, h) for h in range(hpm)])
    for h in range(hpm):
        pltpu.make_async_copy(back.at[place, h], got.at[:, lanes_at(h)], back_recv).start()

    pltpu.make_async_copy(got, got, back_recv).wait()
    out_ref[...] = (got[...].astype(F32) * gate_s[...]).astype(BF)

    if away:
        gone(seen.at[pl.ds(0, len(away))], send_sem.at[GATES])

    @pl.when(feeds_rim)
    def _():
        for i, (_, dst, _) in enumerate(streams):
            gone(dst.at[pl.ds(0, len(away) * rows + team * RIM), :], send_sem.at[i])

    @pl.when(jnp.logical_not(feeds_rim))
    def _():
        for i, (_, dst, _) in enumerate(streams):
            if away:
                gone(dst.at[pl.ds(0, len(away) * rows), :], send_sem.at[i])

    @pl.when(jnp.logical_not(last))
    def _():
        gone(back, back_send)

    @pl.when(last)
    def _():
        if away:
            gone(back.at[pl.ds(0, len(away))], back_send)


def per_device(
    n, q_raw, k_raw, v_raw, gate_z, beta_logit, decay_in, conv_q, conv_k, conv_v, a_log, dt_bias, norm_gain
):
    size = norm_gain.shape[0]
    rows, width = q_raw.shape
    vwidth = v_raw.shape[1]
    heads = vwidth // size
    taps = conv_q.shape[0]
    team = math.gcd(n, width // size)
    kw, vw = width // team, vwidth // team
    kpm, hpm = kw // size, vw // size
    units = team * hpm
    long = RIM + team * rows
    grows = -(-2 * hpm // 8) * 8
    dma = pltpu.SemaphoreType.DMA
    return pl.pallas_call(
        functools.partial(mixer_kernel, "context", "tensor", n, team, size),
        out_shape=pltpu.VMEM((rows, vwidth), BF),
        in_specs=[pl.BlockSpec(memory_space=pltpu.HBM)] * 12,
        out_specs=pl.BlockSpec(memory_space=pltpu.VMEM),
        scratch_shapes=[
            pltpu.VMEM((rows, vwidth), BF),
            pltpu.VMEM((rows, vwidth), F32),
            pltpu.VMEM((rows, vwidth), BF),
            pltpu.VMEM((rows, width), BF),
            pltpu.VMEM((rows, width), BF),
            pltpu.VMEM((rows, vwidth), BF),
            pltpu.VMEM((long, kw), BF),
            pltpu.VMEM((long, kw), BF),
            pltpu.VMEM((long, vw), BF),
            pltpu.VMEM((2, heads, rows), F32),
            pltpu.VMEM((team, grows, rows), F32),
            pltpu.VMEM((team, grows, rows), F32),
            pltpu.VMEM((2 * kpm + hpm, taps, size), BF),
            pltpu.VMEM((2, 1, heads), F32),
            pltpu.VMEM((1, size), F32),
            pltpu.VMEM((long, kw), F32),
            pltpu.VMEM((long, kw), F32),
            pltpu.VMEM((long, vw), F32),
            pltpu.VMEM((units, size, size), BF),
            pltpu.VMEM((units, size), F32),
            pltpu.VMEM((units, size, size), F32),
            pltpu.VMEM((units, rows, rows), F32),
            pltpu.VMEM((units, rows, rows), F32),
            pltpu.VMEM((units, rows, rows), BF),
            pltpu.VMEM((units, size, size), BF),
            pltpu.VMEM((units, rows, size), BF),
            pltpu.VMEM((units, rows, size), F32),
            pltpu.VMEM((hpm, size, size), BF),
            pltpu.VMEM((hpm, size, size), BF),
            pltpu.VMEM((team, hpm, rows, size), BF),
            dma((7,)),
            dma((4,)),
            dma((5,)),
            dma((hpm,)),
            dma,
            dma,
            pltpu.SemaphoreType.REGULAR,
            pltpu.SemaphoreType.REGULAR,
        ],
        compiler_params=pltpu.CompilerParams(
            collective_id=0, has_side_effects=True, vmem_limit_bytes=60 << 20
        ),
        name="mixer",
    )(
        q_raw, k_raw, v_raw, beta_logit.T, decay_in.T, conv_q, conv_k, conv_v,
        a_log[None], dt_bias[None], norm_gain[None], gate_z,
    )


def solution(mesh):
    rows = P(("groups", "context"), "tensor")
    return jax.shard_map(
        functools.partial(per_device, mesh.shape["context"]),
        mesh=mesh,
        in_specs=(rows,) * 6 + (P(None, "tensor"),) * 3 + (P("tensor"),) * 2 + (P(),),
        out_specs=rows,
        check_vma=False,
    )
```

```python
import functools
import math

import jax
import jax.numpy as jnp
from jax import lax
from jax.experimental import pallas as pl
from jax.experimental.pallas import tpu as pltpu
from jax.sharding import PartitionSpec as P

MESH = pl.DeviceIdType.MESH
HIGH = lax.Precision.HIGHEST
RIM = 16
BF = jnp.bfloat16
F32 = jnp.float32


def mm(a, b):
    return jnp.dot(a.astype(BF), b.astype(BF), preferred_element_type=F32)


def mm_nt(a, b):
    return lax.dot_general(a.astype(BF), b.astype(BF), (((1,), (1,)), ((), ())), preferred_element_type=F32)


def conv_silu(full, weights, count):
    taps = weights.shape[0]
    total = weights[0:1].astype(F32) * full(0)
    for i in range(1, taps):
        total = total + weights[i : i + 1].astype(F32) * full(i)
    return (total * jax.nn.sigmoid(total)).astype(BF)


def norm(block):
    block = block.astype(F32)
    return 1.0 / jnp.sqrt(jnp.sum(block * block, axis=-1, keepdims=True) + 1e-06)


def masks(rows):
    row = lax.broadcasted_iota(jnp.int32, (rows, rows), 0)
    col = lax.broadcasted_iota(jnp.int32, (rows, rows), 1)
    return row, col


def halves(a, step):
    parts = [a[i : i + step] for i in range(0, a.shape[0], step)]
    return jnp.concatenate(parts[::2], axis=0), jnp.concatenate(parts[1::2], axis=0)


def less(a, change, step):
    if change.shape[0] == a.shape[0]:
        return a - change
    parts = []
    for i in range(0, a.shape[0], 2 * step):
        parts += [a[i : i + step], a[i + step : i + 2 * step] - change[i // 2 : i // 2 + step]]
    return jnp.concatenate(parts, axis=0)


def unit_scales(blocks):
    size = blocks[0].shape[1]
    down, along = jnp.ones((2 * size, blocks[0].shape[0]), BF), jnp.ones((8, 2 * size), BF)
    columns, lines = [], []
    for block in blocks:
        block = block.astype(F32)
        square = block * block
        high = square.astype(BF)
        both = jnp.concatenate([high, (square - high.astype(F32)).astype(BF)], axis=1)
        columns.append(lax.rsqrt(mm(both, down) + 1e-06))
        lines.append(lax.rsqrt(mm_nt(along, both)[:1] + 1e-06))
    return columns, lines


def key_stage(ks, weights, scales, repeat):
    rows = ks[0].shape[0]
    row, col = masks(rows)
    kn, kn_rows = unit_scales(ks)
    inner = [mm_nt(k, k) * c * r for k, c, r in zip(ks, kn, kn_rows)]
    lower = [weights[u] * inner[u // repeat] for u in range(weights.shape[0])]
    eye = (row == col).astype(F32)
    apart = row ^ col
    inv, rest = [], []
    for h, m in enumerate(lower):
        edge, full = jnp.where(apart == 1, m, 0.0), m + eye
        inv.append(((eye - edge) * scales[h : h + 1]).astype(BF))
        rest.append(full - mm(edge, full))
    step = 2
    while step < rows:
        mask = (apart >= step) & (apart < 2 * step)
        for h in range(len(lower)):
            edge = jnp.where(mask, rest[h], 0.0)
            if step >= 16:
                edge = halves(edge, step)[1]
            if 2 * step < rows:
                both = mm(edge, jnp.concatenate([inv[h], rest[h].astype(BF)], axis=1))
                inv[h], rest[h] = less(inv[h], both[:, :rows].astype(BF), step), less(rest[h], both[:, rows:], step)
            else:
                inv[h] = less(inv[h], mm(edge, inv[h]).astype(BF), step)
        step *= 2
    return kn_rows, inv


def mixer_kernel(
    axis, side, n, team, size,
    q_ref, k_ref, v_ref, bl_ref, di_ref, wq_ref, wk_ref, wv_ref, al_ref, dt_ref, gain_ref, gate_ref,
    out_ref,
    gate_own, gate_s, got,    q_own, k_own, v_own, q_rows, k_rows, v_rows, logits, gates, seen, taps_s, scales, gain,
    fq, fk, fv, m_s, g_s, b_s, r_s, l_s, t_s, s_s, p_s, o_s, held, sent, back,
    local_sem, send_sem, recv_sem, rim_send, hop_send, hop_recv, back_send, back_recv, rim_ready, hop_ready,
):
    me = lax.axis_index(axis)
    place, turn = lax.rem(me, team), me // team
    base = turn * team
    rows = q_ref.shape[0]
    taps = wq_ref.shape[0]
    kw, vw = wq_ref.shape[1] // team, wv_ref.shape[1] // team
    kpm, hpm = kw // size, vw // size
    repeat = hpm // kpm
    units = team * hpm
    first, last = turn == 0, turn == n // team - 1
    tail_place = place == team - 1
    feeds_rim = tail_place & jnp.logical_not(last)
    streams = ((k_own, k_rows, kw), (v_own, v_rows, vw), (q_own, q_rows, kw))
    plans = ((k_rows, 0, fk, kpm), (v_rows, kpm, fv, hpm), (q_rows, kpm + hpm, fq, kpm))
    GATES, TAPS = 3, 4
    core = lax.axis_index(side)
    if team == 4:
        order = [3 - place, lax.rem(place + 2, team), place + 1 - 2 * lax.rem(place, 2), place]
    else:
        order = [lax.rem(place + d, team) for d in range(1, team)] + [place]
    away = order[:-1]

    def lanes_of(who, width):
        return pl.ds(pl.multiple_of(who * width, width), width)

    def rows_of(who):
        return pl.ds(pl.multiple_of(RIM + who * rows, RIM), rows)

    def remote(src, dst, send, recv, to):
        return pltpu.make_async_remote_copy(
            src_ref=src, dst_ref=dst, send_sem=send, recv_sem=recv, device_id=to, device_id_type=MESH
        )

    def loaded(i):
        pltpu.make_async_copy(streams[i][0], streams[i][0], local_sem.at[3 + i]).wait()

    def spread(i):
        src, dst, width = streams[i]
        if i < 2:
            loaded(i)
        for who in away:
            remote(
                src.at[:, lanes_of(who, width)], dst.at[rows_of(place), :],
                send_sem.at[i], recv_sem.at[i], {axis: base + who},
            ).start()
        pltpu.make_async_copy(src.at[:, lanes_of(place, width)], dst.at[rows_of(place), :], recv_sem.at[i]).start()

    def gone(ref, sem):
        pltpu.make_async_copy(ref, ref, sem).wait()

    def left(i):
        gone(streams[i][1].at[pl.ds(RIM, len(away) * rows), :], send_sem.at[i])

    def tap_pieces():
        pieces = []
        at = 0
        for ref, count in ((wk_ref, kpm), (wv_ref, hpm), (wq_ref, kpm)):
            for c in range(count):
                lanes = pl.ds(pl.multiple_of((place * count + c) * size, size), size)
                pieces.append((ref.at[:, lanes], taps_s.at[at]))
                at += 1
        return pieces

    loads = [
        (bl_ref, logits.at[0], 0), (di_ref, logits.at[1], 0), (al_ref, scales.at[0], 1), (dt_ref, scales.at[1], 1),
        (gain_ref, gain, 2), (k_ref, k_own, 3), (v_ref, v_own, 4), (q_ref, q_own, 5),
        (gate_ref, gate_own, 6),
    ]
    barrier = pltpu.get_barrier_semaphore()

    def greet(to):
        pl.semaphore_signal(barrier, inc=1, device_id=to, device_id_type=MESH)

    for who in away:
        greet({axis: base + who})

    @pl.when(jnp.logical_not(last))
    def _():
        greet({axis: me + team})

    @pl.when(feeds_rim)
    def _():
        for p in range(team):
            greet({axis: base + team + p})

    for src, dst, i in loads:
        pltpu.make_async_copy(src, dst, local_sem.at[i]).start()
    for src, dst in tap_pieces():
        pltpu.make_async_copy(src, dst, recv_sem.at[TAPS]).start()

    pltpu.make_async_copy(logits, logits, local_sem.at[0]).wait()
    pltpu.make_async_copy(scales, scales, local_sem.at[1]).wait()
    heads = bl_ref.shape[0]
    diag = lax.broadcasted_iota(jnp.int32, (heads, heads), 0) == lax.broadcasted_iota(jnp.int32, (heads, heads), 1)

    def upright(row):
        return jnp.sum(jnp.where(diag, row, 0.0), axis=1, keepdims=True)

    row, col = masks(rows)
    x = logits[1] + upright(scales[1])
    decay = -jnp.exp(upright(scales[0])) * (jnp.maximum(x, 0.0) + jnp.log1p(jnp.exp(-jnp.abs(x))))
    cum = jnp.dot(decay, (row <= col).astype(F32), precision=HIGH, preferred_element_type=F32)
    beta = jax.nn.sigmoid(logits[0])
    for p in range(team):
        gates[p, pl.ds(0, hpm), :] = cum[p * hpm : (p + 1) * hpm]
        gates[p, pl.ds(hpm, hpm), :] = beta[p * hpm : (p + 1) * hpm]
    pl.semaphore_wait(barrier, len(away) + jnp.where(first, 0, 2))

    @pl.when(jnp.logical_not(first))
    def _():
        pl.semaphore_signal(rim_ready, inc=1, device_id={axis: base - 1}, device_id_type=MESH)
        pl.semaphore_signal(hop_ready, inc=1, device_id={axis: me - team}, device_id_type=MESH)

    for who in away:
        remote(gates.at[who], seen.at[place], send_sem.at[GATES], recv_sem.at[GATES], {axis: base + who}).start()
    pltpu.make_async_copy(gates.at[place], seen.at[place], recv_sem.at[GATES]).start()
    spread(0)

    spread(1)
    loaded(2)
    pltpu.make_async_copy(gate_own, gate_own, local_sem.at[6]).wait()
    gate_s[...] = jax.nn.silu(gate_own[...].astype(F32))

    def rim(p, i):
        src, dst, width = streams[i]
        return remote(
            src.at[pl.ds(rows - RIM, RIM), pl.ds(p * width, width)], dst.at[pl.ds(0, RIM), :],
            rim_send.at[i], recv_sem.at[i], {axis: base + team + p},
        )

    @pl.when(feeds_rim)
    def _():
        pl.semaphore_wait(rim_ready, team)
        for i in range(len(streams)):
            for p in range(team):
                rim(p, i).start()

    @pl.when(first)
    def _():
        for _, dst, _ in streams:
            dst[pl.ds(0, RIM), :] = jnp.zeros((RIM, dst.shape[1]), BF)

    def arrived(ref, i):
        pltpu.make_async_copy(ref, ref, recv_sem.at[i]).wait()

    def stream(i):
        src, at, f_ref, count = plans[i]

        @pl.when(first)
        def _():
            arrived(src.at[pl.ds(RIM, team * rows), :], i)

        @pl.when(jnp.logical_not(first))
        def _():
            arrived(src, i)

        f_ref[...] = src[...].astype(F32)
        parts = []
        for b in range(team):
            for c in range(count):
                lanes = pl.ds(c * size, size)
                parts.append(
                    conv_silu(
                        lambda i: f_ref[pl.ds(RIM - taps + 1 + i + b * rows, rows), lanes], taps_s[at + c], rows
                    )
                )
        return parts

    arrived(seen, GATES)
    pl.when((core == 0) | jnp.logical_not(first))(functools.partial(spread, 2))
    cum_rows = jnp.concatenate([seen[b, pl.ds(0, hpm), :] for b in range(team)], axis=0)
    beta_rows = jnp.concatenate([seen[b, pl.ds(hpm, hpm), :] for b in range(team)], axis=0)
    pad = jnp.zeros((rows - 2 * units, rows), F32)
    columns = jnp.concatenate([cum_rows, beta_rows, pad], axis=0).T
    cum, beta = columns[:, :units], columns[:, units : 2 * units]
    growth = jnp.exp(cum)
    for u in range(units):
        ratio = jnp.exp(jnp.minimum(cum[:, u : u + 1] - cum_rows[u : u + 1], 0.0))
        r_s[u] = jnp.where(row >= col, ratio, 0.0)
        l_s[u] = jnp.where(row > col, ratio * beta[:, u : u + 1], 0.0)
    arrived(taps_s, TAPS)
    ks = stream(0)
    kn_rows, inv = key_stage(ks, l_s, beta_rows, repeat)
    pl.when((core == 1) & first)(functools.partial(spread, 2))
    gain_rows = []
    for u in range(units):
        j = u // repeat
        t_s[u] = inv[u]
        gain_rows.append(jnp.exp(cum_rows[u : u + 1]) * kn_rows[j])
    drawn = [k.astype(F32).T for k in ks]
    ends = []
    for u in range(units):
        j = u // repeat
        tail_row = jnp.exp(cum_rows[u : u + 1, rows - 1 : rows] - cum_rows[u : u + 1])
        ends.append(mm(drawn[j] * (kn_rows[j] * tail_row), t_s[u]))
        g_s[pl.ds(u, 1), :] = jnp.broadcast_to(growth[rows - 1 : rows, u : u + 1], (1, size))
    for u in range(units):
        m_s[u] = (-mm(ends[u] * gain_rows[u], ks[u // repeat])).astype(BF)
    ends = [end.astype(BF) for end in ends]
    vs = stream(1)
    for u in range(units):
        b_s[u] = mm(ends[u], vs[u])

    def hop(h, to):
        return remote(sent.at[h], held.at[h], hop_send, hop_recv.at[h], {axis: to})

    def onward(h, state):
        @pl.when(jnp.logical_not(last))
        def _():
            sent[h] = state.astype(BF)
            if h == 0:
                pl.semaphore_wait(hop_ready, 1)
            hop(h, me + team).start()

    @pl.when(first)
    def _():
        states = [b_s[h] for h in range(hpm)]
        for h in range(hpm):
            s_s[h] = jnp.zeros((size, size), BF)
        for b in range(1, team):
            for h in range(hpm):
                u = b * hpm + h
                low = states[h].astype(BF)
                s_s[u] = low
                states[h] = (
                    b_s[u] + g_s[pl.ds(u, 1), :] * states[h] + jnp.dot(m_s[u], low, preferred_element_type=F32)
                )
        for h in range(hpm):
            onward(h, states[h])

    qs = stream(2)
    qn = [norm(q) * size ** (-0.5) for q in qs]
    cross = [mm_nt(q, k) * c * r for q, k, c, r in zip(qs, ks, qn, kn_rows)]
    reads = [mm(r_s[u] * cross[u // repeat], t_s[u]) for u in range(units)]
    for u in range(units):
        j = u // repeat
        p_s[u] = (qs[j].astype(F32) * (qn[j] * growth[:, u : u + 1]) - mm(reads[u] * gain_rows[u], ks[j])).astype(BF)
        o_s[u] = mm(reads[u], vs[u])

    @pl.when(jnp.logical_not(first))
    def _():
        row, col = masks(size)
        eye = (row == col).astype(F32)
        turns = [g_s[pl.ds(h, 1), :] * eye + m_s[h].astype(F32) for h in range(hpm)]
        adds = [b_s[h] for h in range(hpm)]
        for b in range(1, team):
            for h in range(hpm):
                u = b * hpm + h
                low = jnp.concatenate([turns[h].astype(BF), adds[h].astype(BF)], axis=1)
                end = g_s[pl.ds(u, 1), :]
                moved = jnp.dot(m_s[u], low, preferred_element_type=F32)
                viewed = jnp.dot(p_s[u], low, preferred_element_type=F32)
                p_s[u] = viewed[:, :size].astype(BF)
                o_s[u] = o_s[u] + viewed[:, size:]
                turns[h] = end * turns[h] + moved[:, :size]
                adds[h] = b_s[u] + end * adds[h] + moved[:, size:]
        for h in range(hpm):
            m_s[h] = turns[h].astype(BF)
            b_s[h] = adds[h]

    pltpu.make_async_copy(gain_ref, gain, local_sem.at[2]).wait()
    ones = jnp.ones((2 * size, size), BF)
    def finish(pairs):
        mixed = [
            o_s[b * hpm + h] + jnp.dot(p_s[b * hpm + h], s_s[b * hpm + h], preferred_element_type=F32)
            for b, h in pairs
        ]
        squares = [x * x for x in mixed]
        heads_up = [x.astype(BF) for x in squares]
        rests = [(x - y.astype(F32)).astype(BF) for x, y in zip(squares, heads_up)]
        means = [mm(jnp.concatenate([x, y], axis=1), ones) * (1.0 / size) for x, y in zip(heads_up, rests)]
        for (b, h), x, mean in zip(pairs, mixed, means):
            back[b, h] = (x * lax.rsqrt(mean + 1e-06) * gain[...]).astype(BF)

    def lanes_at(h):
        return pl.ds(pl.multiple_of(place * vw + h * size, size), size)

    for h in range(hpm):

        @pl.when(jnp.logical_not(first))
        def _():
            hop(h, me - team).wait_recv()

            @pl.when(jnp.logical_not(last))
            def _():
                onward(h, b_s[h] + jnp.dot(m_s[h], held[h], preferred_element_type=F32))

            for b in range(team):
                s_s[b * hpm + h] = held[h]

        if away:
            finish([(b, h) for b in away])
        for b in away:
            remote(back.at[b, h], got.at[:, lanes_at(h)], back_send, back_recv, {axis: base + b}).start()

    finish([(place, h) for h in range(hpm)])
    for h in range(hpm):
        out_ref[:, lanes_at(h)] = (back[place, h].astype(F32) * gate_s[:, lanes_at(h)]).astype(BF)

    if away:
        gone(got.at[:, pl.ds(0, len(away) * vw)], back_recv)
    for who in away:
        lanes = pl.ds(pl.multiple_of(who * vw, vw), vw)
        out_ref[:, lanes] = (got[:, lanes].astype(F32) * gate_s[:, lanes]).astype(BF)

    if away:
        gone(back.at[pl.ds(0, len(away))], back_send)
        gone(seen.at[pl.ds(0, len(away))], send_sem.at[GATES])
        for i in range(len(streams)):
            left(i)

    @pl.when(feeds_rim)
    def _():
        for i, (_, dst, _) in enumerate(streams):
            gone(dst.at[pl.ds(RIM, team * RIM), :], rim_send.at[i])

    @pl.when(jnp.logical_not(last))
    def _():
        gone(sent, hop_send)


def per_device(
    n, q_raw, k_raw, v_raw, gate_z, beta_logit, decay_in, conv_q, conv_k, conv_v, a_log, dt_bias, norm_gain
):
    size = norm_gain.shape[0]
    rows, width = q_raw.shape
    vwidth = v_raw.shape[1]
    heads = vwidth // size
    taps = conv_q.shape[0]
    team = math.gcd(n, width // size)
    kw, vw = width // team, vwidth // team
    kpm, hpm = kw // size, vw // size
    units = team * hpm
    long = RIM + team * rows
    grows = -(-2 * hpm // 8) * 8
    dma = pltpu.SemaphoreType.DMA
    return pl.pallas_call(
        functools.partial(mixer_kernel, "context", "tensor", n, team, size),
        out_shape=pltpu.VMEM((rows, vwidth), BF),
        in_specs=[pl.BlockSpec(memory_space=pltpu.HBM)] * 12,
        out_specs=pl.BlockSpec(memory_space=pltpu.VMEM),
        scratch_shapes=[
            pltpu.VMEM((rows, vwidth), BF),
            pltpu.VMEM((rows, vwidth), F32),
            pltpu.VMEM((rows, vwidth), BF),
            pltpu.VMEM((rows, width), BF),
            pltpu.VMEM((rows, width), BF),
            pltpu.VMEM((rows, vwidth), BF),
            pltpu.VMEM((long, kw), BF),
            pltpu.VMEM((long, kw), BF),
            pltpu.VMEM((long, vw), BF),
            pltpu.VMEM((2, heads, rows), F32),
            pltpu.VMEM((team, grows, rows), F32),
            pltpu.VMEM((team, grows, rows), F32),
            pltpu.VMEM((2 * kpm + hpm, taps, size), BF),
            pltpu.VMEM((2, 1, heads), F32),
            pltpu.VMEM((1, size), F32),
            pltpu.VMEM((long, kw), F32),
            pltpu.VMEM((long, kw), F32),
            pltpu.VMEM((long, vw), F32),
            pltpu.VMEM((units, size, size), BF),
            pltpu.VMEM((units, size), F32),
            pltpu.VMEM((units, size, size), F32),
            pltpu.VMEM((units, rows, rows), F32),
            pltpu.VMEM((units, rows, rows), F32),
            pltpu.VMEM((units, rows, rows), BF),
            pltpu.VMEM((units, size, size), BF),
            pltpu.VMEM((units, rows, size), BF),
            pltpu.VMEM((units, rows, size), F32),
            pltpu.VMEM((hpm, size, size), BF),
            pltpu.VMEM((hpm, size, size), BF),
            pltpu.VMEM((team, hpm, rows, size), BF),
            dma((7,)),
            dma((4,)),
            dma((5,)),
            dma((3,)),
            dma,
            dma((hpm,)),
            dma,
            dma,
            pltpu.SemaphoreType.REGULAR,
            pltpu.SemaphoreType.REGULAR,
        ],
        compiler_params=pltpu.CompilerParams(
            collective_id=0, has_side_effects=True, vmem_limit_bytes=60 << 20
        ),
        name="mixer",
    )(
        q_raw, k_raw, v_raw, beta_logit.T, decay_in.T, conv_q, conv_k, conv_v,
        a_log[None], dt_bias[None], norm_gain[None], gate_z,
    )


def solution(mesh):
    rows = P(("groups", "context"), "tensor")
    return jax.shard_map(
        functools.partial(per_device, mesh.shape["context"]),
        mesh=mesh,
        in_specs=(rows,) * 6 + (P(None, "tensor"),) * 3 + (P("tensor"),) * 2 + (P(),),
        out_specs=rows,
        check_vma=False,
    )
```
